32 devices in a mesh: chan: 8 (over z, y), tm: 4 (over x, core).
Axes of the slice: x: 2, y: 2, z: 4, core: 2. Of those that a mesh axis runs over, the one named last changes fastest.
Arguments:
- record: bfloat16 [96, 2048], P('chan', 'tm'), may hold values from -6 to 6
- fir: float32 [96, 65], P('chan'), may hold values from -0.75 to 0.75
Outputs:
- xcorr: float32 [4, 96, 96, 256], P('tm', 'chan')
The draws below stay inside these ranges and needn't reach their ends.
All inputs are finite; a program needn't handle non-finite values.
Results may differ from the reference program's by a relative error of at most 0.004.
Values may be sent and summed in bfloat16 or wider, within the bound.
A program may use at most 64 MiB of HBM per device.

```python
import math
import jax
import jax.numpy as jnp
from jax import lax

CHANNELS = 96
GROUP = 512
GROUPS = 4
SAMPLES = 2048
MAXLAG = 128
HALF = 32
TAPS = 65


def steps_of(own_key, dims, pieces, low, largest):
    factor_of, own = 1.0, jax.random.fold_in(own_key, 6)
    for axis_at, blocks in pieces:
        heights = jnp.exp(jax.random.uniform(jax.random.fold_in(own, axis_at), (blocks,), jnp.float32, low / len(pieces), largest / len(pieces)))
        factor_of = factor_of * jnp.repeat(heights, dims[axis_at] // blocks).reshape([-1 if axis == axis_at else 1 for axis in range(len(dims))])
    return factor_of


def gaussian(stream_key, dims, width, most, cuts=(), held_as=jnp.bfloat16):
    factor_of = steps_of(stream_key, dims, cuts, -0.22, 0.18) if cuts else 1.0
    entries = jax.random.normal(stream_key, dims, jnp.float32) * width * factor_of
    return jnp.minimum(jnp.maximum(entries, -most), most).astype(held_as)


def setup_inputs(seed: int = 0) -> dict:
    streams_of = jax.random.split(jax.random.key(seed), 3)
    return {
        "record": gaussian(streams_of[0], (CHANNELS, SAMPLES), 1.0, 6.0, ((0, 8), (1, 4))),
        "fir": gaussian(streams_of[1], (CHANNELS, TAPS), TAPS ** -0.5, 0.75, ((0, 8),), jnp.float32),
    }


def whiten(record, fir):
    widened = jnp.pad(record.astype(jnp.float32), ((0, 0), (HALF, HALF)))
    length = record.shape[1]
    running = jnp.zeros((record.shape[0], length), jnp.float32)
    for k in range(2 * HALF + 1):
        running = running + fir[:, k:k + 1] * widened[:, k:k + length]
    return running.astype(jnp.bfloat16)

def reference(record, fir):
    whitened = whiten(record, fir)
    padded = jnp.pad(whitened.astype(jnp.float32), ((0, 0), (MAXLAG, MAXLAG)))
    span = GROUP + 2 * MAXLAG
    factor = 1.0 / math.sqrt(GROUP)

    def one_group(number):
        offset = (number * GROUP).astype(jnp.int32)
        window = lax.dynamic_slice_in_dim(padded, offset, span, 1)
        leading = window[:, MAXLAG:MAXLAG + GROUP]
        first = jnp.fft.rfft(leading, n=span)
        second = jnp.fft.rfft(window, n=span)
        spectrum = jnp.conj(first)[:, None, :] * second[None, :, :]
        return jnp.fft.irfft(spectrum, n=span)[:, :, :2 * MAXLAG] * factor
    return lax.map(one_group, jnp.arange(GROUPS, dtype=jnp.int32))
```

```python
import math

import jax
import jax.numpy as jnp
from jax import lax
from jax.experimental import pallas as pl
from jax.experimental.pallas import tpu as pltpu
from jax.sharding import PartitionSpec as P

GROUP = 512
MAXLAG = 128
LAGS = 2 * MAXLAG
SPAN = GROUP + LAGS
BAND = GROUP + MAXLAG
TILE = 128
ROWS = 16
MESH = pl.DeviceIdType.MESH


def spread(taps):
    rows, count = taps.shape
    taps = jnp.concatenate([taps, jnp.zeros((rows, TILE - count), jnp.float32)], axis=1)
    high = taps.astype(jnp.bfloat16).astype(jnp.float32)
    lane = lax.broadcasted_iota(jnp.int32, taps.shape, 1)
    both = [
        jnp.concatenate([jnp.where(lane == k, part, 0.0) for part in (high, taps - high)], axis=1)
        for k in range(count)
    ]
    both = jnp.concatenate(both, axis=0).astype(jnp.bfloat16)
    ones = jnp.ones((2 * TILE, TILE), jnp.bfloat16)
    out = jnp.dot(both, ones, preferred_element_type=jnp.float32)
    return [out[k * rows : (k + 1) * rows] for k in range(count)]


def whiten(x, taps):
    width, count, steps = x.shape[1], taps.shape[1], 8
    taps = [jnp.concatenate([tap] * (width // TILE), axis=1) for tap in spread(taps)]
    moved = [x if b == 0 else pltpu.roll(x, width - b, 1) for b in range(steps)]
    total = None
    for a in range(0, count, steps):
        part = None
        for b in range(min(steps, count - a)):
            term = taps[a + b] * moved[b]
            part = term if part is None else part + term
        if a:
            part = pltpu.roll(part, width - a, 1)
        total = part if total is None else total + part
    return total


def turn(x, lanes):
    return pltpu.roll(x, lanes % TILE, 1)


def pack(tile, edge, half, side):
    row = lax.broadcasted_iota(jnp.int32, (8, TILE), 0)
    lane = lax.broadcasted_iota(jnp.int32, (8, TILE), 1)
    lane = TILE - 1 - lane if side < 0 else lane
    top, low = edge[:8], edge[8:]
    first = pltpu.roll(top, 4, 0)
    second = turn(top, side * half)
    third = turn(pltpu.roll(low, 4, 0), 2 * side * half)
    packed = jnp.where(lane < half, first, jnp.where(lane < 2 * half, second, third))
    return jnp.concatenate([tile[:8], jnp.where(row < 4, tile[8:], packed)], axis=0)


def unpack(tile, half, side):
    row = lax.broadcasted_iota(jnp.int32, (8, TILE), 0)
    lane = lax.broadcasted_iota(jnp.int32, (8, TILE), 1)
    lane = TILE - 1 - lane if side < 0 else lane
    low = tile[8:]
    up = pltpu.roll(low, 4, 0)
    top = jnp.where(row < 4, up, turn(low, -side * half))
    low = turn(up, -2 * side * half)
    inside = lane < half
    return jnp.concatenate([jnp.where(inside, top, 0.0), jnp.where(inside, low, 0.0)], axis=0)


def gather_kernel(record_hbm, fir_hbm, wide, bands, record, fir, mine, full, blocks, near,
                  load, send, recv, ready, beside):
    n, tn = lax.axis_size("chan"), lax.axis_size("tm")
    me, tm = lax.axis_index("chan"), lax.axis_index("tm")
    ch, length = record.shape
    tiles = length // TILE
    half = (fir.shape[1] - 1) // 2
    first, last = tm == 0, tm == tn - 1
    there = (jnp.logical_not(first), jnp.logical_not(last))
    step = (-1, 1, 0)
    mirror = (1, 0, 2)

    get_record = pltpu.make_async_copy(record_hbm, record, load.at[0])
    get_fir = pltpu.make_async_copy(fir_hbm, fir, load.at[1])
    get_record.start()
    get_fir.start()

    def each(d, act):
        if d < 2:
            pl.when(there[d])(act)
        else:
            act()

    def loop(low, high, act, sides=(0, 1, 2)):
        def body(c, carry):
            for d in sides:
                act(c, d)
            return carry
        lax.fori_loop(low, high, body, 0)

    barrier = pltpu.get_barrier_semaphore()

    def signal(sem, c, d):
        each(d, lambda: pl.semaphore_signal(
            sem, inc=1, device_id=(c, tm + step[d]), device_id_type=MESH))

    signal(barrier, me, 1)
    loop(me + 1, n, lambda c, d: signal(barrier, c, d))

    sides = 1 + jnp.minimum(tm, 1) + jnp.minimum(tn - 1 - tm, 1)
    earlier = jnp.minimum(tm, 1) + me * sides

    @pl.when(earlier > 0)
    def _():
        pl.semaphore_wait(barrier, earlier)

    signal(beside, me, 0)
    loop(0, me, lambda c, d: signal(ready.at[me], c, d), (2,))

    @pl.when(first)
    def _():
        near[0] = jnp.zeros(near.shape[1:], near.dtype)

    @pl.when(last)
    def _():
        near[1] = jnp.zeros(near.shape[1:], near.dtype)

    get_record.wait()
    get_fir.wait()
    pad = ROWS - ch
    taps = jnp.concatenate([fir[...], jnp.zeros((pad, fir.shape[1]), jnp.float32)], axis=0)
    x = jnp.concatenate([record[...].astype(jnp.float32), jnp.zeros((pad, length), jnp.float32)], axis=0)
    x = jnp.concatenate([x, jnp.zeros((ROWS, TILE), jnp.float32)], axis=1)
    y = whiten(pltpu.roll(x, half, 1), taps)

    edge = y[:, length:]
    lane = lax.broadcasted_iota(jnp.int32, edge.shape, 1)
    lost = ((lane < half) & last) | ((lane >= TILE - half) & first)
    edge = jnp.where(lost, 0.0, edge)
    parts = [y[:, k * TILE : (k + 1) * TILE] for k in range(tiles)]
    parts[0] = pack(parts[0], edge, half, -1)
    parts[-1] = pack(parts[-1], edge, half, 1)
    mine[...] = jnp.concatenate(parts, axis=0).astype(jnp.bfloat16)

    def copy(c, d, slot):
        if d == 0:
            source, target = mine.at[:ROWS], near.at[1, slot]
        elif d == 1:
            source, target = mine.at[(tiles - 1) * ROWS :], near.at[0, slot]
        else:
            source, target = mine, blocks.at[slot]
        return pltpu.make_async_remote_copy(
            source, target, send.at[d, c], recv.at[mirror[d], slot],
            device_id=(c, tm + step[d]), device_id_type=MESH,
        )

    def up(c, slot):
        return pltpu.make_async_remote_copy(
            full.at[me], full.at[slot], send.at[2, c], recv.at[2, slot],
            device_id=(c, tm), device_id_type=MESH,
        )

    def start(c, d):
        each(d, lambda: copy(c, d, me).start())

    def arrived(c, d):
        each(d, lambda: copy(c, mirror[d], c).wait_recv())

    start(me, 0)
    loop(0, me, start)

    @pl.when(there[1])
    def _():
        pl.semaphore_wait(beside, 1)

    start(me, 1)

    def tile(ref, k):
        return ref[k * ROWS : (k + 1) * ROWS, :].astype(jnp.float32)

    def joined(block, left, right):
        own = [tile(block, k) for k in range(tiles)]
        line = [left + unpack(own[0], half, -1)] + own + [right + unpack(own[-1], half, 1)]
        line[1] = line[1] + unpack(left, half, 1)
        line[-2] = line[-2] + unpack(right, half, -1)
        return line

    arrived(me, 0)
    arrived(me, 1)
    line = joined(mine, tile(near.at[0, me], 0), tile(near.at[1, me], 0))
    full[me] = jnp.concatenate([part[:ch] for part in line], axis=0).astype(jnp.bfloat16)

    def climb(c, carry):
        pl.semaphore_wait(ready.at[c], 1)
        up(c, me).start()
        return carry

    lax.fori_loop(me + 1, n, climb, 0)

    lead = jnp.concatenate(line[1 : tiles + 1] + [jnp.zeros((ROWS, MAXLAG), jnp.float32)], axis=1)
    for i in range(ch):
        line = jnp.broadcast_to(lead[i : i + 1, :], (MAXLAG, BAND))
        moved = pltpu.roll(line, 0, 1, stride=1, stride_axis=0)
        bands[i * MAXLAG : (i + 1) * MAXLAG, :] = moved.astype(jnp.bfloat16)

    for c in range(n):
        @pl.when(c < me)
        def _():
            up(c, c).wait_recv()

        @pl.when(c <= me)
        def _():
            block = full[c].astype(jnp.float32)
            for k in range(tiles + 2):
                wide[c * ch : (c + 1) * ch, k * TILE : (k + 1) * TILE] = block[k * ch : (k + 1) * ch]

        @pl.when(c > me)
        def _():
            for d in range(3):
                arrived(c, d)
            line = joined(blocks.at[c], tile(near.at[0, c], 0), tile(near.at[1, c], 0))
            for k in range(tiles + 2):
                wide[c * ch : (c + 1) * ch, k * TILE : (k + 1) * TILE] = line[k][:ch]

    def sent(c, d):
        each(d, lambda: copy(c, d, me).wait_send())

    loop(0, me, sent)
    sent(me, 0)
    sent(me, 1)

    def drained(c, carry):
        up(c, me).wait_send()
        return carry

    lax.fori_loop(me + 1, n, drained, 0)


def correlate_kernel(wide, bands, out, result, sem):
    rows = wide.shape[0]
    ch = bands.shape[0] // MAXLAG
    factor = 1.0 / math.sqrt(GROUP)
    w = wide[...].astype(jnp.bfloat16)
    both = jnp.concatenate([w[:, :BAND], w[:, MAXLAG:]], axis=0)
    copies = []
    for p in range(ch // 2):
        r = lax.dot_general(
            both, bands[p * LAGS : (p + 1) * LAGS, :], (((1,), (1,)), ((), ())),
            preferred_element_type=jnp.float32,
        ) * factor
        for s in range(2):
            for h in range(2):
                result[2 * p + s, :, h * MAXLAG : (h + 1) * MAXLAG] = r[
                    h * rows : (h + 1) * rows, s * MAXLAG : (s + 1) * MAXLAG
                ]
        copy = pltpu.make_async_copy(
            result.at[2 * p : 2 * p + 2], out.at[0, 2 * p : 2 * p + 2], sem.at[p]
        )
        copy.start()
        copies.append(copy)
    for copy in copies:
        copy.wait()


def local(record, fir):
    ch, length = record.shape
    n = lax.axis_size("chan")
    vmem = pl.BlockSpec(memory_space=pltpu.VMEM)
    hbm = pl.BlockSpec(memory_space=pltpu.HBM)
    tiles = length // TILE
    wide, bands = pl.pallas_call(
        gather_kernel,
        out_shape=(
            pltpu.VMEM((n * ch, SPAN), jnp.float32),
            pltpu.VMEM((ch * MAXLAG, BAND), jnp.bfloat16),
        ),
        in_specs=[hbm, hbm],
        out_specs=(vmem, vmem),
        scratch_shapes=[
            pltpu.VMEM((ch, length), jnp.bfloat16),
            pltpu.VMEM(fir.shape, jnp.float32),
            pltpu.VMEM((tiles * ROWS, TILE), jnp.bfloat16),
            pltpu.VMEM((n, (tiles + 2) * ch, TILE), jnp.bfloat16),
            pltpu.VMEM((n, tiles * ROWS, TILE), jnp.bfloat16),
            pltpu.VMEM((2, n, ROWS, TILE), jnp.bfloat16),
            pltpu.SemaphoreType.DMA((2,)),
            pltpu.SemaphoreType.DMA((3, n)),
            pltpu.SemaphoreType.DMA((3, n)),
            pltpu.SemaphoreType.REGULAR((n,)),
            pltpu.SemaphoreType.REGULAR,
        ],
        compiler_params=pltpu.CompilerParams(
            collective_id=0, has_side_effects=True, vmem_limit_bytes=16 << 20
        ),
    )(*(pltpu.with_memory_space_constraint(x, pltpu.HBM) for x in (record, fir)))
    return pl.pallas_call(
        correlate_kernel,
        out_shape=jax.ShapeDtypeStruct((1, ch, n * ch, LAGS), jnp.float32),
        in_specs=[vmem, vmem],
        out_specs=pl.BlockSpec(memory_space=pl.ANY),
        scratch_shapes=[
            pltpu.VMEM((ch, n * ch, LAGS), jnp.float32),
            pltpu.SemaphoreType.DMA((ch // 2,)),
        ],
        compiler_params=pltpu.CompilerParams(vmem_limit_bytes=16 << 20),
    )(wide, bands)


def solution(mesh):
    in_specs = (P("chan", "tm"), P("chan", None))
    out_specs = P("tm", "chan", None, None)
    return jax.shard_map(local, mesh=mesh, in_specs=in_specs, out_specs=out_specs, check_vma=False)
```

```python
import math

import jax
import jax.numpy as jnp
from jax import lax
from jax.experimental import pallas as pl
from jax.experimental.pallas import tpu as pltpu
from jax.sharding import PartitionSpec as P

GROUP = 512
MAXLAG = 128
LAGS = 2 * MAXLAG
SPAN = GROUP + LAGS
BAND = GROUP + MAXLAG
TILE = 128
ROWS = 16
MESH = pl.DeviceIdType.MESH


def spread(taps):
    rows, count = taps.shape
    taps = jnp.concatenate([taps, jnp.zeros((rows, TILE - count), jnp.float32)], axis=1)
    high = taps.astype(jnp.bfloat16).astype(jnp.float32)
    lane = lax.broadcasted_iota(jnp.int32, taps.shape, 1)
    both = [
        jnp.concatenate([jnp.where(lane == k, part, 0.0) for part in (high, taps - high)], axis=1)
        for k in range(count)
    ]
    both = jnp.concatenate(both, axis=0).astype(jnp.bfloat16)
    ones = jnp.ones((2 * TILE, TILE), jnp.bfloat16)
    out = jnp.dot(both, ones, preferred_element_type=jnp.float32)
    return [out[k * rows : (k + 1) * rows] for k in range(count)]


def whiten(x, taps):
    width, count, steps = x.shape[1], taps.shape[1], 8
    taps = [jnp.concatenate([tap] * (width // TILE), axis=1) for tap in spread(taps)]
    moved = [x if b == 0 else pltpu.roll(x, width - b, 1) for b in range(steps)]
    total = None
    for a in range(0, count, steps):
        part = None
        for b in range(min(steps, count - a)):
            term = taps[a + b] * moved[b]
            part = term if part is None else part + term
        if a:
            part = pltpu.roll(part, width - a, 1)
        total = part if total is None else total + part
    return total


def turn(x, lanes):
    return pltpu.roll(x, lanes % TILE, 1)


def pack(tile, edge, half, side):
    row = lax.broadcasted_iota(jnp.int32, (8, TILE), 0)
    lane = lax.broadcasted_iota(jnp.int32, (8, TILE), 1)
    lane = TILE - 1 - lane if side < 0 else lane
    top, low = edge[:8], edge[8:]
    first = pltpu.roll(top, 4, 0)
    second = turn(top, side * half)
    third = turn(pltpu.roll(low, 4, 0), 2 * side * half)
    packed = jnp.where(lane < half, first, jnp.where(lane < 2 * half, second, third))
    return jnp.concatenate([tile[:8], jnp.where(row < 4, tile[8:], packed)], axis=0)


def unpack(tile, half, side):
    row = lax.broadcasted_iota(jnp.int32, (8, TILE), 0)
    lane = lax.broadcasted_iota(jnp.int32, (8, TILE), 1)
    lane = TILE - 1 - lane if side < 0 else lane
    low = tile[8:]
    up = pltpu.roll(low, 4, 0)
    top = jnp.where(row < 4, up, turn(low, -side * half))
    low = turn(up, -2 * side * half)
    inside = lane < half
    return jnp.concatenate([jnp.where(inside, top, 0.0), jnp.where(inside, low, 0.0)], axis=0)


def correlate(w, bands, out, done=None):
    rows = w.shape[0]
    ch = out.shape[0]
    factor = 1.0 / math.sqrt(GROUP)
    both = jnp.concatenate([w[:, :BAND], w[:, MAXLAG:]], axis=0)
    for p in range(ch // 2):
        r = jnp.dot(
            both, bands[:, p * LAGS : (p + 1) * LAGS], preferred_element_type=jnp.float32
        ) * factor
        for s in range(2):
            for h in range(2):
                out[2 * p + s, :, h * MAXLAG : (h + 1) * MAXLAG] = r[
                    h * rows : (h + 1) * rows, s * MAXLAG : (s + 1) * MAXLAG
                ]
        if done is not None:
            done(p)


def gather_kernel(record_hbm, fir_hbm, result, rest, bands, record, fir, mine, full, blocks, near,
                  load, send, recv, ready, beside):
    n, tn = lax.axis_size("chan"), lax.axis_size("tm")
    me, tm = lax.axis_index("chan"), lax.axis_index("tm")
    ch, length = record.shape
    tiles = length // TILE
    half = (fir.shape[1] - 1) // 2
    first, last = tm == 0, tm == tn - 1
    there = (jnp.logical_not(first), jnp.logical_not(last))
    step = (-1, 1, 0)
    mirror = (1, 0, 2)

    get_record = pltpu.make_async_copy(record_hbm, record, load.at[0])
    get_fir = pltpu.make_async_copy(fir_hbm, fir, load.at[1])
    get_record.start()
    get_fir.start()

    def each(d, act):
        if d < 2:
            pl.when(there[d])(act)
        else:
            act()

    def loop(low, high, act, sides=(0, 1, 2)):
        def body(c, carry):
            for d in sides:
                act(c, d)
            return carry
        lax.fori_loop(low, high, body, 0)

    barrier = pltpu.get_barrier_semaphore()

    def signal(sem, c, d):
        each(d, lambda: pl.semaphore_signal(
            sem, inc=1, device_id=(c, tm + step[d]), device_id_type=MESH))

    signal(barrier, me, 1)
    loop(me + 1, n, lambda c, d: signal(barrier, c, d))

    sides = 1 + jnp.minimum(tm, 1) + jnp.minimum(tn - 1 - tm, 1)
    earlier = jnp.minimum(tm, 1) + me * sides

    @pl.when(earlier > 0)
    def _():
        pl.semaphore_wait(barrier, earlier)

    signal(beside, me, 0)
    loop(0, me, lambda c, d: signal(ready.at[me], c, d), (2,))

    @pl.when(first)
    def _():
        near[0] = jnp.zeros(near.shape[1:], near.dtype)

    @pl.when(last)
    def _():
        near[1] = jnp.zeros(near.shape[1:], near.dtype)

    get_record.wait()
    get_fir.wait()
    pad = ROWS - ch
    taps = jnp.concatenate([fir[...], jnp.zeros((pad, fir.shape[1]), jnp.float32)], axis=0)
    x = jnp.concatenate([record[...].astype(jnp.float32), jnp.zeros((pad, length), jnp.float32)], axis=0)
    x = jnp.concatenate([x, jnp.zeros((ROWS, TILE), jnp.float32)], axis=1)
    y = whiten(pltpu.roll(x, half, 1), taps)

    edge = y[:, length:]
    lane = lax.broadcasted_iota(jnp.int32, edge.shape, 1)
    lost = ((lane < half) & last) | ((lane >= TILE - half) & first)
    edge = jnp.where(lost, 0.0, edge)
    parts = [y[:, k * TILE : (k + 1) * TILE] for k in range(tiles)]
    parts[0] = pack(parts[0], edge, half, -1)
    parts[-1] = pack(parts[-1], edge, half, 1)
    mine[...] = jnp.concatenate(parts, axis=0).astype(jnp.bfloat16)

    def copy(c, d, slot):
        if d == 0:
            source, target = mine.at[:ROWS], near.at[1, slot]
        elif d == 1:
            source, target = mine.at[(tiles - 1) * ROWS :], near.at[0, slot]
        else:
            source, target = mine, blocks.at[slot]
        return pltpu.make_async_remote_copy(
            source, target, send.at[d, c], recv.at[mirror[d], slot],
            device_id=(c, tm + step[d]), device_id_type=MESH,
        )

    def up(c, slot):
        return pltpu.make_async_remote_copy(
            full.at[me], full.at[slot], send.at[2, c], recv.at[2, slot],
            device_id=(c, tm), device_id_type=MESH,
        )

    def start(c, d):
        each(d, lambda: copy(c, d, me).start())

    def arrived(c, d):
        each(d, lambda: copy(c, mirror[d], c).wait_recv())

    start(me, 0)
    loop(0, me, start)

    @pl.when(there[1])
    def _():
        pl.semaphore_wait(beside, 1)

    start(me, 1)

    def tile(ref, k):
        return ref[k * ROWS : (k + 1) * ROWS, :].astype(jnp.float32)

    def joined(block, left, right):
        own = [tile(block, k) for k in range(tiles)]
        line = [left + unpack(own[0], half, -1)] + own + [right + unpack(own[-1], half, 1)]
        line[1] = line[1] + unpack(left, half, 1)
        line[-2] = line[-2] + unpack(right, half, -1)
        return line

    arrived(me, 0)
    arrived(me, 1)
    line = joined(mine, tile(near.at[0, me], 0), tile(near.at[1, me], 0))
    def packed(line):
        return jnp.concatenate([part[:ch] for part in line], axis=0).astype(jnp.bfloat16)

    full[me] = packed(line)

    def climb(low, high):
        def body(c, carry):
            pl.semaphore_wait(ready.at[c], 1)
            up(c, me).start()
            return carry
        lax.fori_loop(jnp.maximum(me + 1, low), high, body, 0)

    middle = n // 2
    lower = me < middle
    climb(0, jnp.where(lower, middle, n))

    flip = lax.broadcasted_iota(jnp.int32, (TILE, TILE), 0) + lax.broadcasted_iota(jnp.int32, (TILE, TILE), 1)
    flip = jnp.where(flip == TILE - 1, 1.0, 0.0).astype(jnp.bfloat16)
    lead = jnp.concatenate(line[1 : tiles + 1], axis=0).astype(jnp.bfloat16)
    lead = jnp.dot(lead, flip, preferred_element_type=jnp.float32)
    below = lax.broadcasted_iota(jnp.int32, (TILE, TILE), 0) >= lax.broadcasted_iota(jnp.int32, (TILE, TILE), 1)
    for i in range(ch):
        before = jnp.zeros((TILE, TILE), jnp.float32)
        for k in range(tiles + 1):
            if k < tiles:
                row = lead[k * ROWS + i : k * ROWS + i + 1, :]
                now = pltpu.roll(jnp.broadcast_to(row, (TILE, TILE)), 1, 1, stride=1, stride_axis=0)
            else:
                now = jnp.zeros((TILE, TILE), jnp.float32)
            bands[k * TILE : (k + 1) * TILE, i * MAXLAG : (i + 1) * MAXLAG] = jnp.where(
                below, now, before
            ).astype(jnp.bfloat16)
            before = now

    climb(jnp.where(lower, middle, n), n - 2)

    def settle(c, carry):
        @pl.when(c < me)
        def _():
            up(c, c).wait_recv()

        @pl.when(c > me)
        def _():
            for d in range(3):
                arrived(c, d)
            full[c] = packed(joined(blocks.at[c], tile(near.at[0, c], 0), tile(near.at[1, c], 0)))

        return carry

    def window(c0):
        lax.fori_loop(c0, c0 + middle, settle, 0)
        held = [full[c0 + q].astype(jnp.float32) for q in range(middle)]
        lines = [
            jnp.concatenate([block[k * ch : (k + 1) * ch] for block in held], axis=0)
            for k in range(tiles + 2)
        ]
        return jnp.concatenate(lines, axis=1).astype(jnp.bfloat16)

    own_half = middle * (me // middle)
    climb(jnp.where(lower, n - 2, n), n)
    correlate(window(own_half), bands, result)
    rest[...] = window(middle - own_half)

    def sent(c, d):
        each(d, lambda: copy(c, d, me).wait_send())

    loop(0, me, sent)
    sent(me, 0)
    sent(me, 1)

    def drained(c, carry):
        up(c, me).wait_send()
        return carry

    lax.fori_loop(me + 1, n, drained, 0)


def finish_kernel(early, rest, bands, out, late, sem):
    ch, rows = early.shape[:2]
    half = lax.axis_index("chan") // (lax.axis_size("chan") // 2)
    here = pl.ds(pl.multiple_of(half * rows, 8), rows)
    there = pl.ds(pl.multiple_of((1 - half) * rows, 8), rows)
    copies = [pltpu.make_async_copy(early, out.at[0, :, here], sem.at[ch // 2])]
    copies[0].start()

    def send(p):
        pair = slice(2 * p, 2 * p + 2)
        copies.append(pltpu.make_async_copy(late.at[pair], out.at[0, pair, there], sem.at[p]))
        copies[-1].start()

    correlate(rest[...], bands, late, send)
    for copy in copies:
        copy.wait()


def local(record, fir):
    ch, length = record.shape
    n = lax.axis_size("chan")
    vmem = pl.BlockSpec(memory_space=pltpu.VMEM)
    hbm = pl.BlockSpec(memory_space=pltpu.HBM)
    tiles = length // TILE
    rows = n // 2 * ch
    held = pl.pallas_call(
        gather_kernel,
        out_shape=(
            pltpu.VMEM((ch, rows, LAGS), jnp.float32),
            pltpu.VMEM((rows, SPAN), jnp.bfloat16),
            pltpu.VMEM((BAND, ch * MAXLAG), jnp.bfloat16),
        ),
        in_specs=[hbm, hbm],
        out_specs=(vmem, vmem, vmem),
        scratch_shapes=[
            pltpu.VMEM((ch, length), jnp.bfloat16),
            pltpu.VMEM(fir.shape, jnp.float32),
            pltpu.VMEM((tiles * ROWS, TILE), jnp.bfloat16),
            pltpu.VMEM((n, (tiles + 2) * ch, TILE), jnp.bfloat16),
            pltpu.VMEM((n, tiles * ROWS, TILE), jnp.bfloat16),
            pltpu.VMEM((2, n, ROWS, TILE), jnp.bfloat16),
            pltpu.SemaphoreType.DMA((2,)),
            pltpu.SemaphoreType.DMA((3, n)),
            pltpu.SemaphoreType.DMA((3, n)),
            pltpu.SemaphoreType.REGULAR((n,)),
            pltpu.SemaphoreType.REGULAR,
        ],
        compiler_params=pltpu.CompilerParams(
            collective_id=0, has_side_effects=True, vmem_limit_bytes=24 << 20
        ),
    )(*(pltpu.with_memory_space_constraint(x, pltpu.HBM) for x in (record, fir)))
    return pl.pallas_call(
        finish_kernel,
        out_shape=jax.ShapeDtypeStruct((1, ch, n * ch, LAGS), jnp.float32),
        in_specs=[vmem, vmem, vmem],
        out_specs=pl.BlockSpec(memory_space=pl.ANY),
        scratch_shapes=[
            pltpu.VMEM((ch, rows, LAGS), jnp.float32),
            pltpu.SemaphoreType.DMA((ch // 2 + 1,)),
        ],
        compiler_params=pltpu.CompilerParams(vmem_limit_bytes=24 << 20),
    )(*held)


def solution(mesh):
    in_specs = (P("chan", "tm"), P("chan", None))
    out_specs = P("tm", "chan", None, None)
    return jax.shard_map(local, mesh=mesh, in_specs=in_specs, out_specs=out_specs, check_vma=False)
```

```python
import math

import jax
import jax.numpy as jnp
from jax import lax
from jax.experimental import pallas as pl
from jax.experimental.pallas import tpu as pltpu
from jax.sharding import PartitionSpec as P

GROUP = 512
MAXLAG = 128
LAGS = 2 * MAXLAG
SPAN = GROUP + LAGS
BAND = GROUP + MAXLAG
TILE = 128
ROWS = 16
NEARER = 4
MESH = pl.DeviceIdType.MESH


def spread(taps):
    rows, count = taps.shape
    taps = jnp.concatenate([taps, jnp.zeros((rows, TILE - count), jnp.float32)], axis=1)
    high = taps.astype(jnp.bfloat16).astype(jnp.float32)
    lane = lax.broadcasted_iota(jnp.int32, taps.shape, 1)
    both = [
        jnp.concatenate([jnp.where(lane == k, part, 0.0) for part in (high, taps - high)], axis=1)
        for k in range(count)
    ]
    both = jnp.concatenate(both, axis=0).astype(jnp.bfloat16)
    ones = jnp.ones((2 * TILE, TILE), jnp.bfloat16)
    out = jnp.dot(both, ones, preferred_element_type=jnp.float32)
    return [out[k * rows : (k + 1) * rows] for k in range(count)]


def whiten(x, taps):
    width, count, steps = x.shape[1], taps.shape[1], 8
    taps = [jnp.concatenate([tap] * (width // TILE), axis=1) for tap in spread(taps)]
    moved = [x if b == 0 else pltpu.roll(x, width - b, 1) for b in range(steps)]
    total = None
    for a in range(0, count, steps):
        part = None
        for b in range(min(steps, count - a)):
            term = taps[a + b] * moved[b]
            part = term if part is None else part + term
        if a:
            part = pltpu.roll(part, width - a, 1)
        total = part if total is None else total + part
    return total


def turn(x, lanes):
    return pltpu.roll(x, lanes % TILE, 1)


def pack(tile, edge, half, side):
    row = lax.broadcasted_iota(jnp.int32, (8, TILE), 0)
    lane = lax.broadcasted_iota(jnp.int32, (8, TILE), 1)
    lane = TILE - 1 - lane if side < 0 else lane
    top, low = edge[:8], edge[8:]
    first = pltpu.roll(top, 4, 0)
    second = turn(top, side * half)
    third = turn(pltpu.roll(low, 4, 0), 2 * side * half)
    packed = jnp.where(lane < half, first, jnp.where(lane < 2 * half, second, third))
    return jnp.concatenate([tile[:8], jnp.where(row < 4, tile[8:], packed)], axis=0)


def unpack(tile, half, side):
    row = lax.broadcasted_iota(jnp.int32, (8, TILE), 0)
    lane = lax.broadcasted_iota(jnp.int32, (8, TILE), 1)
    lane = TILE - 1 - lane if side < 0 else lane
    low = tile[8:]
    up = pltpu.roll(low, 4, 0)
    top = jnp.where(row < 4, up, turn(low, -side * half))
    low = turn(up, -2 * side * half)
    inside = lane < half
    return jnp.concatenate([jnp.where(inside, top, 0.0), jnp.where(inside, low, 0.0)], axis=0)


def correlate(w, bands, out, done=None):
    rows = w.shape[0]
    ch = out.shape[0]
    factor = 1.0 / math.sqrt(GROUP)
    both = jnp.concatenate([w[:, :BAND], w[:, MAXLAG:]], axis=0)
    for p in range(ch // 2):
        r = jnp.dot(
            both, bands[:, p * LAGS : (p + 1) * LAGS], preferred_element_type=jnp.float32
        ) * factor
        for s in range(2):
            for h in range(2):
                out[2 * p + s, :, h * MAXLAG : (h + 1) * MAXLAG] = r[
                    h * rows : (h + 1) * rows, s * MAXLAG : (s + 1) * MAXLAG
                ]
        if done is not None:
            done(p)


def gather_kernel(record_hbm, fir_hbm, result, rest, bands, record, fir, inner, outer, edges, near,
                  load, send, recv, ready, beside):
    n, tn = lax.axis_size("chan"), lax.axis_size("tm")
    me, tm = lax.axis_index("chan"), lax.axis_index("tm")
    ch, length = record.shape
    tiles = length // TILE
    half = (fir.shape[1] - 1) // 2
    first, last = tm == 0, tm == tn - 1
    there = (jnp.logical_not(first), jnp.logical_not(last))
    step = (-1, 1, 0, 0)
    mirror = (1, 0, 2, 3)

    get_record = pltpu.make_async_copy(record_hbm, record, load.at[0])
    get_fir = pltpu.make_async_copy(fir_hbm, fir, load.at[1])
    get_record.start()
    get_fir.start()

    def each(d, act):
        if d < 2:
            pl.when(there[d])(act)
        else:
            act()

    def loop(low, high, act, sides=(0, 1, 2, 3)):
        def body(c, carry):
            for d in sides:
                act(c, d)
            return carry
        lax.fori_loop(low, high, body, 0)

    barrier = pltpu.get_barrier_semaphore()

    def signal(sem, c, d):
        each(d, lambda: pl.semaphore_signal(
            sem, inc=1, device_id=(c, tm + step[d]), device_id_type=MESH))

    signal(barrier, me, 1)
    loop(me + 1, n, lambda c, d: signal(barrier, c, d), (0, 1, 2))

    sides = 1 + jnp.minimum(tm, 1) + jnp.minimum(tn - 1 - tm, 1)
    earlier = jnp.minimum(tm, 1) + me * sides

    @pl.when(earlier > 0)
    def _():
        pl.semaphore_wait(barrier, earlier)

    signal(beside, me, 0)
    loop(0, me, lambda c, d: signal(ready.at[me], c, d), (2,))

    @pl.when(first)
    def _():
        near[0] = jnp.zeros(near.shape[1:], near.dtype)

    @pl.when(last)
    def _():
        near[1] = jnp.zeros(near.shape[1:], near.dtype)

    get_record.wait()
    get_fir.wait()
    pad = ROWS - ch
    taps = jnp.concatenate([fir[...], jnp.zeros((pad, fir.shape[1]), jnp.float32)], axis=0)
    x = jnp.concatenate([record[...].astype(jnp.float32), jnp.zeros((pad, length), jnp.float32)], axis=0)
    x = jnp.concatenate([x, jnp.zeros((ROWS, TILE), jnp.float32)], axis=1)
    y = whiten(pltpu.roll(x, half, 1), taps)

    edge = y[:, length:]
    lane = lax.broadcasted_iota(jnp.int32, edge.shape, 1)
    lost = ((lane < half) & last) | ((lane >= TILE - half) & first)
    edge = jnp.where(lost, 0.0, edge)
    parts = [y[:, k * TILE : (k + 1) * TILE] for k in range(tiles)]
    edges[me, 0] = pack(parts[0], edge, half, -1).astype(jnp.bfloat16)
    edges[me, 1] = pack(parts[-1], edge, half, 1).astype(jnp.bfloat16)
    inner[me] = jnp.concatenate([part[:ch] for part in parts[1:-1]], axis=0).astype(jnp.bfloat16)

    def copy(c, d, slot, complete=False):
        if d < 2:
            source, target = edges.at[me, d], near.at[mirror[d], slot]
        else:
            ref = inner if d == 2 else outer if complete else edges
            source, target = ref.at[me], ref.at[slot]
        return pltpu.make_async_remote_copy(
            source, target, send.at[d, c], recv.at[mirror[d], slot],
            device_id=(c, tm + step[d]), device_id_type=MESH,
        )

    def start(c, d):
        each(d, lambda: copy(c, d, me).start())

    def arrived(c, d, complete=False):
        each(d, lambda: copy(c, mirror[d], c, complete).wait_recv())

    start(me, 0)
    loop(0, me, start)

    @pl.when(there[1])
    def _():
        pl.semaphore_wait(beside, 1)

    start(me, 1)

    def climb(low, high, call, parts):
        def body(c, carry):
            if call:
                pl.semaphore_wait(ready.at[c], 1)
            for d in parts:
                copy(c, d, me, True).start()
            return carry
        lax.fori_loop(low, high, body, 0)

    nearer = jnp.minimum(2 * (me // 2) + NEARER, n)
    climb(me + 1, nearer, True, (2,))

    def tile(ref, k):
        return ref[k].astype(jnp.float32)

    def joined(c):
        left, right = tile(near.at[0], c), tile(near.at[1], c)
        low, high = tile(edges.at[c], 0), tile(edges.at[c], 1)
        line = [
            left + unpack(low, half, -1),
            low + unpack(left, half, 1),
            high + unpack(right, half, -1),
            right + unpack(high, half, 1),
        ]
        outer[c] = jnp.concatenate([part[:ch] for part in line], axis=0).astype(jnp.bfloat16)

    arrived(me, 0)
    arrived(me, 1)
    joined(me)
    climb(me + 1, nearer, False, (3,))
    later = jnp.where(me < 2, jnp.maximum(nearer, n - 2), n)
    climb(nearer, later, True, (2, 3))

    def window(c0, count):
        middle = [inner[c0 + q].astype(jnp.float32) for q in range(count)]
        ends = [outer[c0 + q].astype(jnp.float32) for q in range(count)]

        def rows(blocks, k):
            return jnp.concatenate([block[k * ch : (k + 1) * ch] for block in blocks], axis=0)

        lines = [rows(ends, k) for k in (0, 1)] + [rows(middle, k) for k in range(tiles - 2)]
        return lines + [rows(ends, k) for k in (2, 3)]

    flip = lax.broadcasted_iota(jnp.int32, (TILE, TILE), 0) + lax.broadcasted_iota(jnp.int32, (TILE, TILE), 1)
    flip = jnp.where(flip == TILE - 1, 1.0, 0.0).astype(jnp.bfloat16)
    lead = jnp.concatenate(
        [jnp.concatenate([part, jnp.zeros((pad, TILE), jnp.float32)], axis=0) for part in window(me, 1)[1:-1]], axis=0
    ).astype(jnp.bfloat16)
    lead = jnp.dot(lead, flip, preferred_element_type=jnp.float32)
    below = lax.broadcasted_iota(jnp.int32, (TILE, TILE), 0) >= lax.broadcasted_iota(jnp.int32, (TILE, TILE), 1)
    for i in range(ch):
        before = jnp.zeros((TILE, TILE), jnp.float32)
        for k in range(tiles + 1):
            if k < tiles:
                row = lead[k * ROWS + i : k * ROWS + i + 1, :]
                now = pltpu.roll(jnp.broadcast_to(row, (TILE, TILE)), 1, 1, stride=1, stride_axis=0)
            else:
                now = jnp.zeros((TILE, TILE), jnp.float32)
            bands[k * TILE : (k + 1) * TILE, i * MAXLAG : (i + 1) * MAXLAG] = jnp.where(
                below, now, before
            ).astype(jnp.bfloat16)
            before = now

    climb(later, n, True, (2, 3))

    def settle(c, carry):
        @pl.when(c < me)
        def _():
            arrived(c, 2)
            arrived(c, 3, True)

        @pl.when(c > me)
        def _():
            for d in range(4):
                arrived(c, d)
            joined(c)

        return carry

    middle = n // 2
    own_half = middle * (me // middle)
    lax.fori_loop(own_half, own_half + middle, settle, 0)
    correlate(jnp.concatenate(window(own_half, middle), axis=1).astype(jnp.bfloat16), bands, result)

    def sent(c, d):
        each(d, lambda: copy(c, d, me).wait_send())

    loop(0, me, sent)
    sent(me, 0)
    sent(me, 1)
    loop(me + 1, n, lambda c, d: copy(c, d, me, True).wait_send(), (2, 3))

    other = middle - own_half
    lax.fori_loop(other, other + middle, settle, 0)
    rest[...] = jnp.concatenate(window(other, middle), axis=1).astype(jnp.bfloat16)


def finish_kernel(early, rest, bands, out, late, sem):
    ch, rows = early.shape[:2]
    half = lax.axis_index("chan") // (lax.axis_size("chan") // 2)
    here = pl.ds(pl.multiple_of(half * rows, 8), rows)
    there = pl.ds(pl.multiple_of((1 - half) * rows, 8), rows)
    copies = [pltpu.make_async_copy(early, out.at[0, :, here], sem.at[ch // 2])]
    copies[0].start()

    def send(p):
        pair = slice(2 * p, 2 * p + 2)
        copies.append(pltpu.make_async_copy(late.at[pair], out.at[0, pair, there], sem.at[p]))
        copies[-1].start()

    correlate(rest[...], bands, late, send)
    for copy in copies:
        copy.wait()


def local(record, fir):
    ch, length = record.shape
    n = lax.axis_size("chan")
    vmem = pl.BlockSpec(memory_space=pltpu.VMEM)
    hbm = pl.BlockSpec(memory_space=pltpu.HBM)
    tiles = length // TILE
    rows = n // 2 * ch
    held = pl.pallas_call(
        gather_kernel,
        out_shape=(
            pltpu.VMEM((ch, rows, LAGS), jnp.float32),
            pltpu.VMEM((rows, SPAN), jnp.bfloat16),
            pltpu.VMEM((BAND, ch * MAXLAG), jnp.bfloat16),
        ),
        in_specs=[hbm, hbm],
        out_specs=(vmem, vmem, vmem),
        scratch_shapes=[
            pltpu.VMEM((ch, length), jnp.bfloat16),
            pltpu.VMEM(fir.shape, jnp.float32),
            pltpu.VMEM((n, (tiles - 2) * ch, TILE), jnp.bfloat16),
            pltpu.VMEM((n, 4 * ch, TILE), jnp.bfloat16),
            pltpu.VMEM((n, 2, ROWS, TILE), jnp.bfloat16),
            pltpu.VMEM((2, n, ROWS, TILE), jnp.bfloat16),
            pltpu.SemaphoreType.DMA((2,)),
            pltpu.SemaphoreType.DMA((4, n)),
            pltpu.SemaphoreType.DMA((4, n)),
            pltpu.SemaphoreType.REGULAR((n,)),
            pltpu.SemaphoreType.REGULAR,
        ],
        compiler_params=pltpu.CompilerParams(
            collective_id=0, has_side_effects=True, vmem_limit_bytes=24 << 20
        ),
    )(*(pltpu.with_memory_space_constraint(x, pltpu.HBM) for x in (record, fir)))
    return pl.pallas_call(
        finish_kernel,
        out_shape=jax.ShapeDtypeStruct((1, ch, n * ch, LAGS), jnp.float32),
        in_specs=[vmem, vmem, vmem],
        out_specs=pl.BlockSpec(memory_space=pl.ANY),
        scratch_shapes=[
            pltpu.VMEM((ch, rows, LAGS), jnp.float32),
            pltpu.SemaphoreType.DMA((ch // 2 + 1,)),
        ],
        compiler_params=pltpu.CompilerParams(vmem_limit_bytes=24 << 20),
    )(*held)


def solution(mesh):
    in_specs = (P("chan", "tm"), P("chan", None))
    out_specs = P("tm", "chan", None, None)
    return jax.shard_map(local, mesh=mesh, in_specs=in_specs, out_specs=out_specs, check_vma=False)
```

```python
import math

import jax
import jax.numpy as jnp
from jax import lax
from jax.experimental import pallas as pl
from jax.experimental.pallas import tpu as pltpu
from jax.sharding import PartitionSpec as P

GROUP = 512
MAXLAG = 128
LAGS = 2 * MAXLAG
SPAN = GROUP + LAGS
BAND = GROUP + MAXLAG
TILE = 128
ROWS = 16
NEARER = 4
STEP = 4
MESH = pl.DeviceIdType.MESH


def spread(taps):
    rows, count = taps.shape
    taps = jnp.concatenate([taps, jnp.zeros((rows, TILE - count), jnp.float32)], axis=1)
    high = taps.astype(jnp.bfloat16).astype(jnp.float32)
    lane = lax.broadcasted_iota(jnp.int32, taps.shape, 1)
    both = [
        jnp.concatenate([jnp.where(lane == k, part, 0.0) for part in (high, taps - high)], axis=1)
        for k in range(count)
    ]
    both = jnp.concatenate(both, axis=0).astype(jnp.bfloat16)
    ones = jnp.ones((2 * TILE, TILE), jnp.bfloat16)
    out = jnp.dot(both, ones, preferred_element_type=jnp.float32)
    return [out[k * rows : (k + 1) * rows] for k in range(count)]


def whiten(x, taps, half):
    width, count, steps = x.shape[1], taps.shape[1], 8
    taps = [jnp.concatenate([tap] * (width // TILE), axis=1) for tap in spread(taps)]
    moved = [pltpu.roll(x, (half - b) % width, 1) for b in range(steps)]
    total = None
    for a in range(0, count, steps):
        part = None
        for b in range(min(steps, count - a)):
            term = taps[a + b] * moved[b]
            part = term if part is None else part + term
        if a:
            part = pltpu.roll(part, width - a, 1)
        total = part if total is None else total + part
    return total


def turn(x, lanes):
    return pltpu.roll(x, lanes % TILE, 1)


def pack(tile, edge, half, side):
    row = lax.broadcasted_iota(jnp.int32, (8, TILE), 0)
    lane = lax.broadcasted_iota(jnp.int32, (8, TILE), 1)
    lane = TILE - 1 - lane if side < 0 else lane
    top, low = edge[:8], edge[8:]
    first = pltpu.roll(top, 4, 0)
    second = turn(top, side * half)
    third = turn(pltpu.roll(low, 4, 0), 2 * side * half)
    packed = jnp.where(lane < half, first, jnp.where(lane < 2 * half, second, third))
    return jnp.concatenate([tile[:8], jnp.where(row < 4, tile[8:], packed)], axis=0)


def unpack(tile, half, side):
    row = lax.broadcasted_iota(jnp.int32, (8, TILE), 0)
    lane = lax.broadcasted_iota(jnp.int32, (8, TILE), 1)
    lane = TILE - 1 - lane if side < 0 else lane
    low = tile[8:]
    up = pltpu.roll(low, 4, 0)
    top = jnp.where(row < 4, up, turn(low, -side * half))
    low = turn(up, -2 * side * half)
    inside = lane < half
    return jnp.concatenate([jnp.where(inside, top, 0.0), jnp.where(inside, low, 0.0)], axis=0)


def correlate(w, bands, out, step=2, done=None):
    rows = w.shape[0]
    ch = out.shape[0]
    factor = 1.0 / math.sqrt(GROUP)
    both = jnp.concatenate([w[:, :BAND], w[:, MAXLAG:]], axis=0)
    width = step * MAXLAG
    for p in range(ch // step):
        r = jnp.dot(
            both, bands[:, p * width : (p + 1) * width], preferred_element_type=jnp.float32
        ) * factor
        for s in range(step):
            for h in range(2):
                out[step * p + s, :, h * MAXLAG : (h + 1) * MAXLAG] = r[
                    h * rows : (h + 1) * rows, s * MAXLAG : (s + 1) * MAXLAG
                ]
        if done is not None:
            done(p)


def gather_kernel(record_hbm, fir_hbm, result, rest, bands, record, fir, inner, outer, edges, near,
                  load, send, recv, ready, beside):
    n, tn = lax.axis_size("chan"), lax.axis_size("tm")
    me, tm = lax.axis_index("chan"), lax.axis_index("tm")
    ch, length = record.shape
    tiles = length // TILE
    half = (fir.shape[1] - 1) // 2
    first, last = tm == 0, tm == tn - 1
    there = (jnp.logical_not(first), jnp.logical_not(last))
    step = (-1, 1, 0, 0)
    mirror = (1, 0, 2, 3)

    get_record = pltpu.make_async_copy(record_hbm, record, load.at[0])
    get_fir = pltpu.make_async_copy(fir_hbm, fir, load.at[1])
    get_record.start()
    get_fir.start()

    def each(d, act):
        if d < 2:
            pl.when(there[d])(act)
        else:
            act()

    def loop(low, high, act, sides=(0, 1, 2, 3)):
        def body(c, carry):
            for d in sides:
                act(c, d)
            return carry
        lax.fori_loop(low, high, body, 0)

    barrier = pltpu.get_barrier_semaphore()

    def signal(sem, c, d):
        each(d, lambda: pl.semaphore_signal(
            sem, inc=1, device_id=(c, tm + step[d]), device_id_type=MESH))

    signal(barrier, me, 1)
    loop(me + 1, n, lambda c, d: signal(barrier, c, d), (0, 1, 2))

    sides = 1 + jnp.minimum(tm, 1) + jnp.minimum(tn - 1 - tm, 1)
    earlier = jnp.minimum(tm, 1) + me * sides

    @pl.when(earlier > 0)
    def _():
        pl.semaphore_wait(barrier, earlier)

    signal(beside, me, 0)
    loop(0, me, lambda c, d: signal(ready.at[me], c, d), (2,))

    @pl.when(first)
    def _():
        near[0] = jnp.zeros(near.shape[1:], near.dtype)

    @pl.when(last)
    def _():
        near[1] = jnp.zeros(near.shape[1:], near.dtype)

    get_record.wait()
    get_fir.wait()
    pad = ROWS - ch
    taps = jnp.concatenate([fir[...], jnp.zeros((pad, fir.shape[1]), jnp.float32)], axis=0)
    x = jnp.concatenate([record[...].astype(jnp.float32), jnp.zeros((pad, length), jnp.float32)], axis=0)
    x = jnp.concatenate([x, jnp.zeros((ROWS, TILE), jnp.float32)], axis=1)
    y = whiten(x, taps, half)

    edge = y[:, length:]
    lane = lax.broadcasted_iota(jnp.int32, edge.shape, 1)
    lost = ((lane < half) & last) | ((lane >= TILE - half) & first)
    edge = jnp.where(lost, 0.0, edge)
    parts = [y[:, k * TILE : (k + 1) * TILE] for k in range(tiles)]
    edges[me, 0] = pack(parts[0], edge, half, -1).astype(jnp.bfloat16)
    edges[me, 1] = pack(parts[-1], edge, half, 1).astype(jnp.bfloat16)
    inner[me] = jnp.concatenate([part[:ch] for part in parts[1:-1]], axis=0).astype(jnp.bfloat16)

    def copy(c, d, slot, complete=False):
        if d < 2:
            source, target = edges.at[me, d], near.at[mirror[d], slot]
        else:
            ref = inner if d == 2 else outer if complete else edges
            source, target = ref.at[me], ref.at[slot]
        return pltpu.make_async_remote_copy(
            source, target, send.at[d, c], recv.at[mirror[d], slot],
            device_id=(c, tm + step[d]), device_id_type=MESH,
        )

    def start(c, d):
        each(d, lambda: copy(c, d, me).start())

    def arrived(c, d, complete=False):
        each(d, lambda: copy(c, mirror[d], c, complete).wait_recv())

    start(me, 0)
    loop(0, me, start)

    @pl.when(there[1])
    def _():
        pl.semaphore_wait(beside, 1)

    start(me, 1)

    def climb(low, high, call, parts):
        def body(c, carry):
            if call:
                pl.semaphore_wait(ready.at[c], 1)
            for d in parts:
                copy(c, d, me, True).start()
            return carry
        lax.fori_loop(low, high, body, 0)

    nearer = jnp.minimum(2 * (me // 2) + NEARER, n)
    climb(me + 1, nearer, True, (2,))

    def tile(ref, k):
        return ref[k].astype(jnp.float32)

    def sums(c):
        left, right = tile(near.at[0], c), tile(near.at[1], c)
        low, high = tile(edges.at[c], 0), tile(edges.at[c], 1)
        return [
            (left + unpack(low, half, -1))[:ch],
            (low + unpack(left, half, 1))[:ch],
            (high + unpack(right, half, -1))[:ch],
            (right + unpack(high, half, 1))[:ch],
        ]

    def joined(c):
        outer[c] = jnp.concatenate(sums(c), axis=0).astype(jnp.bfloat16)

    arrived(me, 0)
    arrived(me, 1)
    joined(me)
    climb(me + 1, nearer, False, (3,))
    later = jnp.where(me < 2, jnp.maximum(nearer, n - 2), n)
    climb(nearer, later, True, (2, 3))

    def window(c0, count):
        middle = [inner[c0 + q].astype(jnp.float32) for q in range(count)]
        ends = [outer[c0 + q].astype(jnp.float32) for q in range(count)]

        def rows(blocks, k):
            return jnp.concatenate([block[k * ch : (k + 1) * ch] for block in blocks], axis=0)

        lines = [rows(ends, k) for k in (0, 1)] + [rows(middle, k) for k in range(tiles - 2)]
        return lines + [rows(ends, k) for k in (2, 3)]

    flip = lax.broadcasted_iota(jnp.int32, (TILE, TILE), 0) + lax.broadcasted_iota(jnp.int32, (TILE, TILE), 1)
    flip = jnp.where(flip == TILE - 1, 1.0, 0.0).astype(jnp.bfloat16)
    lead = jnp.concatenate(
        [jnp.concatenate([part, jnp.zeros((pad, TILE), jnp.float32)], axis=0) for part in window(me, 1)[1:-1]], axis=0
    ).astype(jnp.bfloat16)
    lead = jnp.dot(lead, flip, preferred_element_type=jnp.float32)
    below = lax.broadcasted_iota(jnp.int32, (TILE, TILE), 0) >= lax.broadcasted_iota(jnp.int32, (TILE, TILE), 1)
    for i in range(ch):
        before = jnp.zeros((TILE, TILE), jnp.float32)
        for k in range(tiles + 1):
            if k < tiles:
                row = lead[k * ROWS + i : k * ROWS + i + 1, :]
                now = pltpu.roll(jnp.broadcast_to(row, (TILE, TILE)), 1, 1, stride=1, stride_axis=0)
            else:
                now = jnp.zeros((TILE, TILE), jnp.float32)
            bands[k * TILE : (k + 1) * TILE, i * MAXLAG : (i + 1) * MAXLAG] = jnp.where(
                below, now, before
            ).astype(jnp.bfloat16)
            before = now

    climb(later, n, True, (2, 3))

    def settle(c, low, high):
        @pl.when(c < me)
        def _():
            arrived(c, 2)
            arrived(c, 3, True)
            low(c)

        @pl.when(c > me)
        def _():
            for d in range(4):
                arrived(c, d)
            high(c)

    def settle_own(c, carry):
        settle(c, lambda c: None, joined)
        return carry

    middle = n // 2
    own_half = middle * (me // middle)
    lax.fori_loop(own_half, own_half + middle, settle_own, 0)
    correlate(jnp.concatenate(window(own_half, middle), axis=1).astype(jnp.bfloat16), bands, result)

    def sent(c, d):
        each(d, lambda: copy(c, d, me).wait_send())

    loop(0, me, sent)
    sent(me, 0)
    sent(me, 1)
    loop(me + 1, n, lambda c, d: copy(c, d, me, True).wait_send(), (2, 3))

    other = middle - own_half
    for q in range(middle):
        def put(block, places, q=q):
            for part, k in zip(block, places):
                rest[q * ch : (q + 1) * ch, k * TILE : (k + 1) * TILE] = part

        ends, between = (0, 1, tiles, tiles + 1), range(2, tiles)

        def rows(ref, c, count):
            block = ref[c].astype(jnp.float32)
            return [block[k * ch : (k + 1) * ch] for k in range(count)]

        def low(c):
            put(rows(outer, c, 4), ends)
            put(rows(inner, c, tiles - 2), between)

        def high(c):
            put(rows(inner, c, tiles - 2), between)
            put(sums(c), ends)

        settle(other + q, low, high)


def finish_kernel(early, rest, bands, out, late, sem):
    ch, rows = early.shape[:2]
    half = lax.axis_index("chan") // (lax.axis_size("chan") // 2)
    here = pl.ds(pl.multiple_of(half * rows, 8), rows)
    there = pl.ds(pl.multiple_of((1 - half) * rows, 8), rows)
    copies = [pltpu.make_async_copy(early, out.at[0, :, here], sem.at[ch // STEP])]
    copies[0].start()

    def send(p):
        pair = slice(STEP * p, STEP * p + STEP)
        copies.append(pltpu.make_async_copy(late.at[pair], out.at[0, pair, there], sem.at[p]))
        copies[-1].start()

    correlate(rest[...].astype(jnp.bfloat16), bands, late, STEP, send)
    for copy in copies:
        copy.wait()


def local(record, fir):
    ch, length = record.shape
    n = lax.axis_size("chan")
    vmem = pl.BlockSpec(memory_space=pltpu.VMEM)
    hbm = pl.BlockSpec(memory_space=pltpu.HBM)
    tiles = length // TILE
    rows = n // 2 * ch
    held = pl.pallas_call(
        gather_kernel,
        out_shape=(
            pltpu.VMEM((ch, rows, LAGS), jnp.float32),
            pltpu.VMEM((rows, SPAN), jnp.float32),
            pltpu.VMEM((BAND, ch * MAXLAG), jnp.bfloat16),
        ),
        in_specs=[hbm, hbm],
        out_specs=(vmem, vmem, vmem),
        scratch_shapes=[
            pltpu.VMEM((ch, length), jnp.bfloat16),
            pltpu.VMEM(fir.shape, jnp.float32),
            pltpu.VMEM((n, (tiles - 2) * ch, TILE), jnp.bfloat16),
            pltpu.VMEM((n, 4 * ch, TILE), jnp.bfloat16),
            pltpu.VMEM((n, 2, ROWS, TILE), jnp.bfloat16),
            pltpu.VMEM((2, n, ROWS, TILE), jnp.bfloat16),
            pltpu.SemaphoreType.DMA((2,)),
            pltpu.SemaphoreType.DMA((4, n)),
            pltpu.SemaphoreType.DMA((4, n)),
            pltpu.SemaphoreType.REGULAR((n,)),
            pltpu.SemaphoreType.REGULAR,
        ],
        compiler_params=pltpu.CompilerParams(
            collective_id=0, has_side_effects=True, vmem_limit_bytes=24 << 20
        ),
    )(*(pltpu.with_memory_space_constraint(x, pltpu.HBM) for x in (record, fir)))
    return pl.pallas_call(
        finish_kernel,
        out_shape=jax.ShapeDtypeStruct((1, ch, n * ch, LAGS), jnp.float32),
        in_specs=[vmem, vmem, vmem],
        out_specs=pl.BlockSpec(memory_space=pl.ANY),
        scratch_shapes=[
            pltpu.VMEM((ch, rows, LAGS), jnp.float32),
            pltpu.SemaphoreType.DMA((ch // STEP + 1,)),
        ],
        compiler_params=pltpu.CompilerParams(vmem_limit_bytes=24 << 20),
    )(*held)


def solution(mesh):
    in_specs = (P("chan", "tm"), P("chan", None))
    out_specs = P("tm", "chan", None, None)
    return jax.shard_map(local, mesh=mesh, in_specs=in_specs, out_specs=out_specs, check_vma=False)
```

```python
import math

import jax
import jax.numpy as jnp
from jax import lax
from jax.experimental import pallas as pl
from jax.experimental.pallas import tpu as pltpu
from jax.sharding import PartitionSpec as P

GROUP = 512
MAXLAG = 128
LAGS = 2 * MAXLAG
SPAN = GROUP + LAGS
BAND = GROUP + MAXLAG
TILE = 128
ROWS = 16
NEARER = 4
STEP = 4
TOGETHER = 4
MESH = pl.DeviceIdType.MESH


def spread(taps):
    rows, count = taps.shape
    taps = jnp.concatenate([taps, jnp.zeros((rows, TILE - count), jnp.float32)], axis=1)
    high = taps.astype(jnp.bfloat16).astype(jnp.float32)
    lane = lax.broadcasted_iota(jnp.int32, taps.shape, 1)
    both = [
        jnp.concatenate([jnp.where(lane == k, part, 0.0) for part in (high, taps - high)], axis=1)
        for k in range(count)
    ]
    both = jnp.concatenate(both, axis=0).astype(jnp.bfloat16)
    ones = jnp.ones((2 * TILE, TILE), jnp.bfloat16)
    out = jnp.dot(both, ones, preferred_element_type=jnp.float32)
    return [out[k * rows : (k + 1) * rows] for k in range(count)]


def whiten(x, taps, half):
    width, count, steps = x.shape[1], taps.shape[1], 8
    taps = [jnp.concatenate([tap] * (width // TILE), axis=1) for tap in spread(taps)]
    moved = [pltpu.roll(x, (half - b) % width, 1) for b in range(steps)]
    total = None
    for a in range(0, count, steps):
        part = None
        for b in range(min(steps, count - a)):
            term = taps[a + b] * moved[b]
            part = term if part is None else part + term
        if a:
            part = pltpu.roll(part, width - a, 1)
        total = part if total is None else total + part
    return total


def turn(x, lanes):
    return pltpu.roll(x, lanes % TILE, 1)


def pack(tile, edge, half, side):
    row = lax.broadcasted_iota(jnp.int32, (8, TILE), 0)
    lane = lax.broadcasted_iota(jnp.int32, (8, TILE), 1)
    lane = TILE - 1 - lane if side < 0 else lane
    top, low = edge[:8], edge[8:]
    first = pltpu.roll(top, 4, 0)
    second = turn(top, side * half)
    third = turn(pltpu.roll(low, 4, 0), 2 * side * half)
    packed = jnp.where(lane < half, first, jnp.where(lane < 2 * half, second, third))
    return jnp.concatenate([tile[:8], jnp.where(row < 4, tile[8:], packed)], axis=0)


def unpack(tile, half, side):
    row = lax.broadcasted_iota(jnp.int32, (8, TILE), 0)
    lane = lax.broadcasted_iota(jnp.int32, (8, TILE), 1)
    lane = TILE - 1 - lane if side < 0 else lane
    low = tile[8:]
    up = pltpu.roll(low, 4, 0)
    top = jnp.where(row < 4, up, turn(low, -side * half))
    low = turn(up, -2 * side * half)
    inside = lane < half
    return jnp.concatenate([jnp.where(inside, top, 0.0), jnp.where(inside, low, 0.0)], axis=0)


def correlate(w, bands, out, step=2, done=None):
    rows = w.shape[0]
    ch = out.shape[0]
    factor = 1.0 / math.sqrt(GROUP)
    both = jnp.concatenate([w[:, :BAND], w[:, MAXLAG:]], axis=0)
    width = step * MAXLAG
    for p in range(ch // step):
        r = jnp.dot(
            both, bands[:, p * width : (p + 1) * width], preferred_element_type=jnp.float32
        ) * factor
        for s in range(step):
            for h in range(2):
                out[step * p + s, :, h * MAXLAG : (h + 1) * MAXLAG] = r[
                    h * rows : (h + 1) * rows, s * MAXLAG : (s + 1) * MAXLAG
                ]
        if done is not None:
            done(p)


def gather_kernel(record_hbm, fir_hbm, result, rest, bands, record, fir, inner, outer, edges, near, leads, both,
                  window_up, down_one, down_two, one_edge, two_edges,
                  load, send, recv, ready, beside):
    n, tn = lax.axis_size("chan"), lax.axis_size("tm")
    me, tm = lax.axis_index("chan"), lax.axis_index("tm")
    ch, length = record.shape
    tiles = length // TILE
    half = (fir.shape[1] - 1) // 2
    first, last = tm == 0, tm == tn - 1
    there = (jnp.logical_not(first), jnp.logical_not(last))
    step = (-1, 1, 0, 0)
    mirror = (1, 0, 2, 3)

    get_record = pltpu.make_async_copy(record_hbm, record, load.at[0])
    get_fir = pltpu.make_async_copy(fir_hbm, fir, load.at[1])
    get_record.start()
    get_fir.start()

    def each(d, act):
        if d < 2:
            pl.when(there[d])(act)
        else:
            act()

    def loop(low, high, act, sides=(0, 1, 2, 3)):
        def body(c, carry):
            for d in sides:
                act(c, d)
            return carry
        lax.fori_loop(low, high, body, 0)

    barrier = pltpu.get_barrier_semaphore()

    def signal(sem, c, d):
        each(d, lambda: pl.semaphore_signal(
            sem, inc=1, device_id=(c, tm + step[d]), device_id_type=MESH))

    signal(barrier, me, 1)
    loop(me + 1, n, lambda c, d: signal(barrier, c, d), (0, 1, 2))

    sides = 1 + jnp.minimum(tm, 1) + jnp.minimum(tn - 1 - tm, 1)
    earlier = jnp.minimum(tm, 1) + me * sides

    @pl.when(earlier > 0)
    def _():
        pl.semaphore_wait(barrier, earlier)

    signal(beside, me, 0)
    loop(0, me, lambda c, d: signal(ready.at[me], c, d), (2,))

    @pl.when(first)
    def _():
        near[0] = jnp.zeros(near.shape[1:], near.dtype)

    @pl.when(last)
    def _():
        near[1] = jnp.zeros(near.shape[1:], near.dtype)

    get_record.wait()
    get_fir.wait()
    pad = ROWS - ch
    taps = jnp.concatenate([fir[...], jnp.zeros((pad, fir.shape[1]), jnp.float32)], axis=0)
    x = jnp.concatenate([record[...].astype(jnp.float32), jnp.zeros((pad, length), jnp.float32)], axis=0)
    x = jnp.concatenate([x, jnp.zeros((ROWS, TILE), jnp.float32)], axis=1)
    y = whiten(x, taps, half)

    edge = y[:, length:]
    lane = lax.broadcasted_iota(jnp.int32, edge.shape, 1)
    lost = ((lane < half) & last) | ((lane >= TILE - half) & first)
    edge = jnp.where(lost, 0.0, edge)
    parts = [y[:, k * TILE : (k + 1) * TILE] for k in range(tiles)]
    edges[me, 0] = pack(parts[0], edge, half, -1).astype(jnp.bfloat16)
    edges[me, 1] = pack(parts[-1], edge, half, 1).astype(jnp.bfloat16)
    inner[me] = jnp.concatenate([part[:ch] for part in parts[1:-1]], axis=0).astype(jnp.bfloat16)

    def copy(c, d, slot, complete=False):
        if d < 2:
            source, target = edges.at[me, d], near.at[mirror[d], slot]
        else:
            ref = inner if d == 2 else outer if complete else edges
            source, target = ref.at[me], ref.at[slot]
        return pltpu.make_async_remote_copy(
            source, target, send.at[c], recv.at[slot],
            device_id=(c, tm + step[d]), device_id_type=MESH,
        )

    def start(c, d):
        each(d, lambda: copy(c, d, me).start())

    def took(sem, ref):
        pltpu.make_async_copy(ref, ref, sem).wait()

    def took_sides(sem, one, two):
        pl.when(first | last)(lambda: took(sem, one))
        pl.when(there[0] & there[1])(lambda: took(sem, two))

    start(me, 0)
    loop(0, me, start)

    @pl.when(there[1])
    def _():
        pl.semaphore_wait(beside, 1)

    start(me, 1)

    def climb(low, high, call, parts):
        def body(c, carry):
            if call:
                pl.semaphore_wait(ready.at[c], 1)
            for d in parts:
                copy(c, d, me, True).start()
            return carry
        lax.fori_loop(low, high, body, 0)

    nearer = jnp.minimum(2 * (me // 2) + NEARER, n)
    climb(me + 1, nearer, True, (2,))

    def tile(ref, k):
        return ref[k].astype(jnp.float32)

    def sums(c):
        left, right = tile(near.at[0], c), tile(near.at[1], c)
        low, high = tile(edges.at[c], 0), tile(edges.at[c], 1)
        return [
            (left + unpack(low, half, -1))[:ch],
            (low + unpack(left, half, 1))[:ch],
            (high + unpack(right, half, -1))[:ch],
            (right + unpack(high, half, 1))[:ch],
        ]

    def joined(c):
        outer[c] = jnp.concatenate(sums(c), axis=0).astype(jnp.bfloat16)

    took_sides(recv.at[me], one_edge, two_edges)
    joined(me)
    climb(me + 1, nearer, False, (3,))
    later = jnp.where(me < 2, jnp.maximum(nearer, n - 2), n)
    climb(nearer, later, True, (2, 3))

    def window(c0, count):
        middle = [inner[c0 + q].astype(jnp.float32) for q in range(count)]
        ends = [outer[c0 + q].astype(jnp.float32) for q in range(count)]

        def rows(blocks, k):
            return jnp.concatenate([block[k * ch : (k + 1) * ch] for block in blocks], axis=0)

        lines = [rows(ends, k) for k in (0, 1)] + [rows(middle, k) for k in range(tiles - 2)]
        return lines + [rows(ends, k) for k in (2, 3)]

    flip = lax.broadcasted_iota(jnp.int32, (TILE, TILE), 0) + lax.broadcasted_iota(jnp.int32, (TILE, TILE), 1)
    flip = jnp.where(flip == TILE - 1, 1.0, 0.0).astype(jnp.bfloat16)
    lead = jnp.concatenate(
        [jnp.concatenate([part, jnp.zeros((pad, TILE), jnp.float32)], axis=0) for part in window(me, 1)[1:-1]], axis=0
    ).astype(jnp.bfloat16)
    lead = jnp.dot(lead, flip, preferred_element_type=jnp.float32)
    below = lax.broadcasted_iota(jnp.int32, (TILE, TILE), 0) >= lax.broadcasted_iota(jnp.int32, (TILE, TILE), 1)
    leads[...] = lead

    def spread_channel(i):
        column = pl.ds(pl.multiple_of(i * MAXLAG, MAXLAG), MAXLAG)
        before = jnp.zeros((TILE, TILE), jnp.float32)
        for k in range(tiles + 1):
            if k < tiles:
                row = leads[pl.ds(k * ROWS + i, 1), :]
                now = pltpu.roll(jnp.broadcast_to(row, (TILE, TILE)), 1, 1, stride=1, stride_axis=0)
            else:
                now = jnp.zeros((TILE, TILE), jnp.float32)
            bands[k * TILE : (k + 1) * TILE, column] = jnp.where(below, now, before).astype(jnp.bfloat16)
            before = now

    def spread_channels(step, carry):
        for i in range(TOGETHER):
            spread_channel(TOGETHER * step + i)
        return carry

    lax.fori_loop(0, ch // TOGETHER, spread_channels, 0)

    climb(later, n, True, (2, 3))

    def settle(c, carry):
        @pl.when(c < me)
        def _():
            took(recv.at[c], window_up)

        @pl.when(c > me)
        def _():
            took_sides(recv.at[c], down_one, down_two)
            joined(c)

        return carry

    middle = n // 2
    own_half = middle * (me // middle)
    lax.fori_loop(own_half, own_half + middle, settle, 0)
    rows = middle * ch
    w = jnp.concatenate(window(own_half, middle), axis=1).astype(jnp.bfloat16)
    both[...] = jnp.concatenate([w[:, :BAND], w[:, MAXLAG:]], axis=0)

    width = STEP * MAXLAG

    def correlate_some(p, carry):
        columns = pl.ds(pl.multiple_of(p * width, width), width)
        r = jnp.dot(both[...], bands[:, columns], preferred_element_type=jnp.float32)
        r = r * (1.0 / math.sqrt(GROUP))
        for s in range(STEP):
            for h in range(2):
                result[STEP * p + s, :, h * MAXLAG : (h + 1) * MAXLAG] = r[
                    h * rows : (h + 1) * rows, s * MAXLAG : (s + 1) * MAXLAG
                ]
        return carry

    lax.fori_loop(0, ch // STEP, correlate_some, 0)

    def sent_down(c, carry):
        took_sides(send.at[c], down_one, down_two)
        return carry

    def sent_up(c, carry):
        took(send.at[c], window_up)
        return carry

    lax.fori_loop(0, me, sent_down, 0)
    took_sides(send.at[me], one_edge, two_edges)
    lax.fori_loop(me + 1, n, sent_up, 0)

    other = middle - own_half
    lax.fori_loop(other, other + middle, settle, 0)
    rest[...] = jnp.concatenate(window(other, middle), axis=1).astype(jnp.bfloat16)


def finish_kernel(early, rest, bands, out, late, sem):
    ch, rows = early.shape[:2]
    half = lax.axis_index("chan") // (lax.axis_size("chan") // 2)
    here = pl.ds(pl.multiple_of(half * rows, 8), rows)
    there = pl.ds(pl.multiple_of((1 - half) * rows, 8), rows)
    copies = [pltpu.make_async_copy(early, out.at[0, :, here], sem.at[ch // STEP])]
    copies[0].start()

    def send(p):
        pair = slice(STEP * p, STEP * p + STEP)
        copies.append(pltpu.make_async_copy(late.at[pair], out.at[0, pair, there], sem.at[p]))
        copies[-1].start()

    correlate(rest[...], bands, late, STEP, send)
    for copy in copies:
        copy.wait()


def local(record, fir):
    ch, length = record.shape
    n = lax.axis_size("chan")
    vmem = pl.BlockSpec(memory_space=pltpu.VMEM)
    hbm = pl.BlockSpec(memory_space=pltpu.HBM)
    tiles = length // TILE
    rows = n // 2 * ch
    held = pl.pallas_call(
        gather_kernel,
        out_shape=(
            pltpu.VMEM((ch, rows, LAGS), jnp.float32),
            pltpu.VMEM((rows, SPAN), jnp.bfloat16),
            pltpu.VMEM((BAND, ch * MAXLAG), jnp.bfloat16),
        ),
        in_specs=[hbm, hbm],
        out_specs=(vmem, vmem, vmem),
        scratch_shapes=[
            pltpu.VMEM((ch, length), jnp.bfloat16),
            pltpu.VMEM(fir.shape, jnp.float32),
            pltpu.VMEM((n, (tiles - 2) * ch, TILE), jnp.bfloat16),
            pltpu.VMEM((n, 4 * ch, TILE), jnp.bfloat16),
            pltpu.VMEM((n, 2, ROWS, TILE), jnp.bfloat16),
            pltpu.VMEM((2, n, ROWS, TILE), jnp.bfloat16),
            pltpu.VMEM((tiles * ROWS, TILE), jnp.float32),
            pltpu.VMEM((2 * rows, BAND), jnp.bfloat16),
            pltpu.VMEM(((tiles + 2) * ch, TILE), jnp.bfloat16),
            pltpu.VMEM(((tiles - 2) * ch + 3 * ROWS, TILE), jnp.bfloat16),
            pltpu.VMEM(((tiles - 2) * ch + 4 * ROWS, TILE), jnp.bfloat16),
            pltpu.VMEM((ROWS, TILE), jnp.bfloat16),
            pltpu.VMEM((2 * ROWS, TILE), jnp.bfloat16),
            pltpu.SemaphoreType.DMA((2,)),
            pltpu.SemaphoreType.DMA((n,)),
            pltpu.SemaphoreType.DMA((n,)),
            pltpu.SemaphoreType.REGULAR((n,)),
            pltpu.SemaphoreType.REGULAR,
        ],
        compiler_params=pltpu.CompilerParams(
            collective_id=0, has_side_effects=True, vmem_limit_bytes=24 << 20
        ),
    )(*(pltpu.with_memory_space_constraint(x, pltpu.HBM) for x in (record, fir)))
    return pl.pallas_call(
        finish_kernel,
        out_shape=jax.ShapeDtypeStruct((1, ch, n * ch, LAGS), jnp.float32),
        in_specs=[vmem, vmem, vmem],
        out_specs=pl.BlockSpec(memory_space=pl.ANY),
        scratch_shapes=[
            pltpu.VMEM((ch, rows, LAGS), jnp.float32),
            pltpu.SemaphoreType.DMA((ch // STEP + 1,)),
        ],
        compiler_params=pltpu.CompilerParams(vmem_limit_bytes=24 << 20),
    )(*held)


def solution(mesh):
    in_specs = (P("chan", "tm"), P("chan", None))
    out_specs = P("tm", "chan", None, None)
    return jax.shard_map(local, mesh=mesh, in_specs=in_specs, out_specs=out_specs, check_vma=False)
```

```python
import math

import jax
import jax.numpy as jnp
from jax import lax
from jax.experimental import pallas as pl
from jax.experimental.pallas import tpu as pltpu
from jax.sharding import PartitionSpec as P

GROUP = 512
MAXLAG = 128
LAGS = 2 * MAXLAG
SPAN = GROUP + LAGS
BAND = GROUP + MAXLAG
TILE = 128
ROWS = 16
NEARER = 4
STEP = 4
TOGETHER = 4
MESH = pl.DeviceIdType.MESH


def spread(taps):
    rows, count = taps.shape
    taps = jnp.concatenate([taps, jnp.zeros((rows, TILE - count), jnp.float32)], axis=1)
    high = taps.astype(jnp.bfloat16).astype(jnp.float32)
    lane = lax.broadcasted_iota(jnp.int32, taps.shape, 1)
    both = [
        jnp.concatenate([jnp.where(lane == k, part, 0.0) for part in (high, taps - high)], axis=1)
        for k in range(count)
    ]
    both = jnp.concatenate(both, axis=0).astype(jnp.bfloat16)
    ones = jnp.ones((2 * TILE, TILE), jnp.bfloat16)
    out = jnp.dot(both, ones, preferred_element_type=jnp.float32)
    return [out[k * rows : (k + 1) * rows] for k in range(count)]


def whiten(x, taps, half):
    width, count, steps = x.shape[1], taps.shape[1], 8
    taps = [jnp.concatenate([tap] * (width // TILE), axis=1) for tap in spread(taps)]
    moved = [pltpu.roll(x, (half - b) % width, 1) for b in range(steps)]
    total = None
    for a in range(0, count, steps):
        part = None
        for b in range(min(steps, count - a)):
            term = taps[a + b] * moved[b]
            part = term if part is None else part + term
        if a:
            part = pltpu.roll(part, width - a, 1)
        total = part if total is None else total + part
    return total


def turn(x, lanes):
    return pltpu.roll(x, lanes % TILE, 1)


def pack(tile, edge, half, side):
    row = lax.broadcasted_iota(jnp.int32, (8, TILE), 0)
    lane = lax.broadcasted_iota(jnp.int32, (8, TILE), 1)
    lane = TILE - 1 - lane if side < 0 else lane
    top, low = edge[:8], edge[8:]
    first = pltpu.roll(top, 4, 0)
    second = turn(top, side * half)
    third = turn(pltpu.roll(low, 4, 0), 2 * side * half)
    packed = jnp.where(lane < half, first, jnp.where(lane < 2 * half, second, third))
    return jnp.concatenate([tile[:8], jnp.where(row < 4, tile[8:], packed)], axis=0)


def unpack(tile, half, side):
    row = lax.broadcasted_iota(jnp.int32, (8, TILE), 0)
    lane = lax.broadcasted_iota(jnp.int32, (8, TILE), 1)
    lane = TILE - 1 - lane if side < 0 else lane
    low = tile[8:]
    up = pltpu.roll(low, 4, 0)
    top = jnp.where(row < 4, up, turn(low, -side * half))
    low = turn(up, -2 * side * half)
    inside = lane < half
    return jnp.concatenate([jnp.where(inside, top, 0.0), jnp.where(inside, low, 0.0)], axis=0)


def correlate(w, bands, out, step=2, done=None):
    rows = w.shape[0]
    ch = out.shape[0]
    factor = 1.0 / math.sqrt(GROUP)
    both = jnp.concatenate([w[:, :BAND], w[:, MAXLAG:]], axis=0)
    width = step * MAXLAG
    for p in range(ch // step):
        r = jnp.dot(
            both, bands[:, p * width : (p + 1) * width], preferred_element_type=jnp.float32
        ) * factor
        for s in range(step):
            for h in range(2):
                out[step * p + s, :, h * MAXLAG : (h + 1) * MAXLAG] = r[
                    h * rows : (h + 1) * rows, s * MAXLAG : (s + 1) * MAXLAG
                ]
        if done is not None:
            done(p)


def gather_kernel(record_hbm, fir_hbm, result, rest, bands, record, fir, inner, outer, edges, near, leads, both,
                  window_up, down_one, down_two, one_edge, two_edges,
                  send, recv, ready):
    n, tn = lax.axis_size("chan"), lax.axis_size("tm")
    me, tm = lax.axis_index("chan"), lax.axis_index("tm")
    ch, length = record.shape
    tiles = length // TILE
    half = (fir.shape[1] - 1) // 2
    first, last = tm == 0, tm == tn - 1
    there = (jnp.logical_not(first), jnp.logical_not(last))
    step = (-1, 1, 0, 0)
    mirror = (1, 0, 2, 3)

    get_record = pltpu.make_async_copy(record_hbm, record, send.at[0])
    get_fir = pltpu.make_async_copy(fir_hbm, fir, send.at[1])
    get_record.start()
    get_fir.start()

    def each(d, act):
        if d < 2:
            pl.when(there[d])(act)
        else:
            act()

    def loop(low, high, act, sides=(0, 1, 2, 3)):
        def body(c, carry):
            for d in sides:
                act(c, d)
            return carry
        lax.fori_loop(low, high, body, 0)

    barrier = pltpu.get_barrier_semaphore()

    def signal(sem, c, d):
        each(d, lambda: pl.semaphore_signal(
            sem, inc=1, device_id=(c, tm + step[d]), device_id_type=MESH))

    signal(barrier, me, 1)
    loop(me + 1, n, lambda c, d: signal(barrier, c, d), (0, 1, 2))

    sides = 1 + jnp.minimum(tm, 1) + jnp.minimum(tn - 1 - tm, 1)
    earlier = jnp.minimum(tm, 1) + me * sides

    @pl.when(earlier > 0)
    def _():
        pl.semaphore_wait(barrier, earlier)

    signal(ready.at[me], me, 0)
    loop(0, me, lambda c, d: signal(ready.at[me], c, d), (2,))

    @pl.when(first)
    def _():
        near[0] = jnp.zeros(near.shape[1:], near.dtype)

    @pl.when(last)
    def _():
        near[1] = jnp.zeros(near.shape[1:], near.dtype)

    get_record.wait()
    get_fir.wait()
    pad = ROWS - ch
    taps = jnp.concatenate([fir[...], jnp.zeros((pad, fir.shape[1]), jnp.float32)], axis=0)
    x = jnp.concatenate([record[...].astype(jnp.float32), jnp.zeros((pad, length), jnp.float32)], axis=0)
    x = jnp.concatenate([x, jnp.zeros((ROWS, TILE), jnp.float32)], axis=1)
    y = whiten(x, taps, half)

    edge = y[:, length:]
    lane = lax.broadcasted_iota(jnp.int32, edge.shape, 1)
    lost = ((lane < half) & last) | ((lane >= TILE - half) & first)
    edge = jnp.where(lost, 0.0, edge)
    parts = [y[:, k * TILE : (k + 1) * TILE] for k in range(tiles)]
    edges[me, 0] = pack(parts[0], edge, half, -1).astype(jnp.bfloat16)
    edges[me, 1] = pack(parts[-1], edge, half, 1).astype(jnp.bfloat16)
    inner[me] = jnp.concatenate([part[:ch] for part in parts[1:-1]], axis=0).astype(jnp.bfloat16)

    def copy(c, d, slot, complete=False):
        if d < 2:
            source, target = edges.at[me, d], near.at[mirror[d], slot]
        else:
            ref = inner if d == 2 else outer if complete else edges
            source, target = ref.at[me], ref.at[slot]
        return pltpu.make_async_remote_copy(
            source, target, send.at[c], recv.at[slot],
            device_id=(c, tm + step[d]), device_id_type=MESH,
        )

    def start(c, d):
        each(d, lambda: copy(c, d, me).start())

    def took(sem, ref):
        pltpu.make_async_copy(ref, ref, sem).wait()

    def took_sides(sem, one, two):
        pl.when(first | last)(lambda: took(sem, one))
        pl.when(there[0] & there[1])(lambda: took(sem, two))

    start(me, 0)
    loop(0, me, start)

    @pl.when(there[1])
    def _():
        pl.semaphore_wait(ready.at[me], 1)

    start(me, 1)

    def climb(low, high, call, parts):
        def body(c, carry):
            if call:
                pl.semaphore_wait(ready.at[c], 1)
            for d in parts:
                copy(c, d, me, True).start()
            return carry
        lax.fori_loop(low, high, body, 0)

    nearer = jnp.minimum(2 * (me // 2) + NEARER, n)
    climb(me + 1, nearer, True, (2,))

    def tile(ref, k):
        return ref[k].astype(jnp.float32)

    def sums(c):
        left, right = tile(near.at[0], c), tile(near.at[1], c)
        low, high = tile(edges.at[c], 0), tile(edges.at[c], 1)
        return [
            (left + unpack(low, half, -1))[:ch],
            (low + unpack(left, half, 1))[:ch],
            (high + unpack(right, half, -1))[:ch],
            (right + unpack(high, half, 1))[:ch],
        ]

    def joined(c):
        outer[c] = jnp.concatenate(sums(c), axis=0).astype(jnp.bfloat16)

    took_sides(recv.at[me], one_edge, two_edges)
    joined(me)
    climb(me + 1, nearer, False, (3,))
    later = jnp.where(me < 2, jnp.maximum(nearer, n - 2), n)
    climb(nearer, later, True, (2, 3))

    def window(c0, count):
        middle = [inner[c0 + q].astype(jnp.float32) for q in range(count)]
        ends = [outer[c0 + q].astype(jnp.float32) for q in range(count)]

        def rows(blocks, k):
            return jnp.concatenate([block[k * ch : (k + 1) * ch] for block in blocks], axis=0)

        lines = [rows(ends, k) for k in (0, 1)] + [rows(middle, k) for k in range(tiles - 2)]
        return lines + [rows(ends, k) for k in (2, 3)]

    flip = lax.broadcasted_iota(jnp.int32, (TILE, TILE), 0) + lax.broadcasted_iota(jnp.int32, (TILE, TILE), 1)
    flip = jnp.where(flip == TILE - 1, 1.0, 0.0).astype(jnp.bfloat16)
    lead = jnp.concatenate(
        [jnp.concatenate([part, jnp.zeros((pad, TILE), jnp.float32)], axis=0) for part in window(me, 1)[1:-1]], axis=0
    ).astype(jnp.bfloat16)
    lead = jnp.dot(lead, flip, preferred_element_type=jnp.float32)
    below = lax.broadcasted_iota(jnp.int32, (TILE, TILE), 0) >= lax.broadcasted_iota(jnp.int32, (TILE, TILE), 1)
    leads[...] = lead

    def spread_channel(i):
        column = pl.ds(pl.multiple_of(i * MAXLAG, MAXLAG), MAXLAG)
        before = jnp.zeros((TILE, TILE), jnp.float32)
        for k in range(tiles + 1):
            if k < tiles:
                row = leads[pl.ds(k * ROWS + i, 1), :]
                now = pltpu.roll(jnp.broadcast_to(row, (TILE, TILE)), 1, 1, stride=1, stride_axis=0)
            else:
                now = jnp.zeros((TILE, TILE), jnp.float32)
            bands[k * TILE : (k + 1) * TILE, column] = jnp.where(below, now, before).astype(jnp.bfloat16)
            before = now

    def spread_channels(step, carry):
        for i in range(TOGETHER):
            spread_channel(TOGETHER * step + i)
        return carry

    lax.fori_loop(0, ch // TOGETHER, spread_channels, 0)

    climb(later, n, True, (2, 3))

    def settle(c, carry):
        @pl.when(c < me)
        def _():
            took(recv.at[c], window_up)

        @pl.when(c > me)
        def _():
            took_sides(recv.at[c], down_one, down_two)
            joined(c)

        return carry

    middle = n // 2
    own_half = middle * (me // middle)
    lax.fori_loop(own_half, own_half + middle, settle, 0)
    rows = middle * ch
    w = jnp.concatenate(window(own_half, middle), axis=1).astype(jnp.bfloat16)
    both[...] = jnp.concatenate([w[:, :BAND], w[:, MAXLAG:]], axis=0)

    width = STEP * MAXLAG

    def correlate_some(p, carry):
        columns = pl.ds(pl.multiple_of(p * width, width), width)
        r = jnp.dot(both[...], bands[:, columns], preferred_element_type=jnp.float32)
        r = r * (1.0 / math.sqrt(GROUP))
        for s in range(STEP):
            for h in range(2):
                result[STEP * p + s, :, h * MAXLAG : (h + 1) * MAXLAG] = r[
                    h * rows : (h + 1) * rows, s * MAXLAG : (s + 1) * MAXLAG
                ]
        return carry

    lax.fori_loop(0, ch // STEP, correlate_some, 0)

    def sent_down(c, carry):
        took_sides(send.at[c], down_one, down_two)
        return carry

    def sent_up(c, carry):
        took(send.at[c], window_up)
        return carry

    lax.fori_loop(0, me, sent_down, 0)
    took_sides(send.at[me], one_edge, two_edges)
    lax.fori_loop(me + 1, n, sent_up, 0)

    other = middle - own_half
    lax.fori_loop(other, other + middle, settle, 0)
    rest[...] = jnp.concatenate(window(other, middle), axis=1).astype(jnp.bfloat16)


def finish_kernel(early, rest, bands, out, late, sem):
    ch, rows = early.shape[:2]
    half = lax.axis_index("chan") // (lax.axis_size("chan") // 2)
    here = pl.ds(pl.multiple_of(half * rows, 8), rows)
    there = pl.ds(pl.multiple_of((1 - half) * rows, 8), rows)
    pltpu.make_async_copy(early, out.at[0, :, here], sem).start()

    def send(p):
        pair = slice(STEP * p, STEP * p + STEP)
        pltpu.make_async_copy(late.at[pair], out.at[0, pair, there], sem).start()

    correlate(rest[...], bands, late, STEP, send)
    pltpu.make_async_copy(out, out, sem).wait()


def local(record, fir):
    ch, length = record.shape
    n = lax.axis_size("chan")
    vmem = pl.BlockSpec(memory_space=pltpu.VMEM)
    hbm = pl.BlockSpec(memory_space=pltpu.HBM)
    tiles = length // TILE
    rows = n // 2 * ch
    held = pl.pallas_call(
        gather_kernel,
        out_shape=(
            pltpu.VMEM((ch, rows, LAGS), jnp.float32),
            pltpu.VMEM((rows, SPAN), jnp.bfloat16),
            pltpu.VMEM((BAND, ch * MAXLAG), jnp.bfloat16),
        ),
        in_specs=[hbm, hbm],
        out_specs=(vmem, vmem, vmem),
        scratch_shapes=[
            pltpu.VMEM((ch, length), jnp.bfloat16),
            pltpu.VMEM(fir.shape, jnp.float32),
            pltpu.VMEM((n, (tiles - 2) * ch, TILE), jnp.bfloat16),
            pltpu.VMEM((n, 4 * ch, TILE), jnp.bfloat16),
            pltpu.VMEM((n, 2, ROWS, TILE), jnp.bfloat16),
            pltpu.VMEM((2, n, ROWS, TILE), jnp.bfloat16),
            pltpu.VMEM((tiles * ROWS, TILE), jnp.float32),
            pltpu.VMEM((2 * rows, BAND), jnp.bfloat16),
            pltpu.VMEM(((tiles + 2) * ch, TILE), jnp.bfloat16),
            pltpu.VMEM(((tiles - 2) * ch + 3 * ROWS, TILE), jnp.bfloat16),
            pltpu.VMEM(((tiles - 2) * ch + 4 * ROWS, TILE), jnp.bfloat16),
            pltpu.VMEM((ROWS, TILE), jnp.bfloat16),
            pltpu.VMEM((2 * ROWS, TILE), jnp.bfloat16),
            pltpu.SemaphoreType.DMA((n,)),
            pltpu.SemaphoreType.DMA((n,)),
            pltpu.SemaphoreType.REGULAR((n,)),
        ],
        compiler_params=pltpu.CompilerParams(
            collective_id=0, has_side_effects=True, vmem_limit_bytes=24 << 20
        ),
    )(*(pltpu.with_memory_space_constraint(x, pltpu.HBM) for x in (record, fir)))
    return pl.pallas_call(
        finish_kernel,
        out_shape=jax.ShapeDtypeStruct((1, ch, n * ch, LAGS), jnp.float32),
        in_specs=[vmem, vmem, vmem],
        out_specs=pl.BlockSpec(memory_space=pl.ANY),
        scratch_shapes=[
            pltpu.VMEM((ch, rows, LAGS), jnp.float32),
            pltpu.SemaphoreType.DMA,
        ],
        compiler_params=pltpu.CompilerParams(vmem_limit_bytes=24 << 20),
    )(*held)


def solution(mesh):
    in_specs = (P("chan", "tm"), P("chan", None))
    out_specs = P("tm", "chan", None, None)
    return jax.shard_map(local, mesh=mesh, in_specs=in_specs, out_specs=out_specs, check_vma=False)
```

```python
import math

import jax
import jax.numpy as jnp
from jax import lax
from jax.experimental import pallas as pl
from jax.experimental.pallas import tpu as pltpu
from jax.sharding import PartitionSpec as P

GROUP = 512
MAXLAG = 128
LAGS = 2 * MAXLAG
SPAN = GROUP + LAGS
BAND = GROUP + MAXLAG
TILE = 128
ROWS = 16
NEARER = 4
STEP = 4
TOGETHER = 4
MESH = pl.DeviceIdType.MESH


def spread(taps):
    rows, count = taps.shape
    taps = jnp.concatenate([taps, jnp.zeros((rows, TILE - count), jnp.float32)], axis=1)
    high = taps.astype(jnp.bfloat16).astype(jnp.float32)
    lane = lax.broadcasted_iota(jnp.int32, taps.shape, 1)
    both = [
        jnp.concatenate([jnp.where(lane == k, part, 0.0) for part in (high, taps - high)], axis=1)
        for k in range(count)
    ]
    both = jnp.concatenate(both, axis=0).astype(jnp.bfloat16)
    ones = jnp.ones((2 * TILE, TILE), jnp.bfloat16)
    out = jnp.dot(both, ones, preferred_element_type=jnp.float32)
    return [out[k * rows : (k + 1) * rows] for k in range(count)]


def whiten(x, taps, half):
    width, count, steps = x.shape[1], taps.shape[1], 8
    taps = [jnp.concatenate([tap] * (width // TILE), axis=1) for tap in spread(taps)]
    moved = [pltpu.roll(x, (half - b) % width, 1) for b in range(steps)]
    total = None
    for a in range(0, count, steps):
        part = None
        for b in range(min(steps, count - a)):
            term = taps[a + b] * moved[b]
            part = term if part is None else part + term
        if a:
            part = pltpu.roll(part, width - a, 1)
        total = part if total is None else total + part
    return total


def turn(x, lanes):
    return pltpu.roll(x, lanes % TILE, 1)


def pack(tile, edge, half, side):
    row = lax.broadcasted_iota(jnp.int32, (8, TILE), 0)
    lane = lax.broadcasted_iota(jnp.int32, (8, TILE), 1)
    lane = TILE - 1 - lane if side < 0 else lane
    top, low = edge[:8], edge[8:]
    first = pltpu.roll(top, 4, 0)
    second = turn(top, side * half)
    third = turn(pltpu.roll(low, 4, 0), 2 * side * half)
    packed = jnp.where(lane < half, first, jnp.where(lane < 2 * half, second, third))
    return jnp.concatenate([tile[:8], jnp.where(row < 4, tile[8:], packed)], axis=0)


def unpack(tile, half, side):
    row = lax.broadcasted_iota(jnp.int32, (8, TILE), 0)
    lane = lax.broadcasted_iota(jnp.int32, (8, TILE), 1)
    lane = TILE - 1 - lane if side < 0 else lane
    low = tile[8:]
    up = pltpu.roll(low, 4, 0)
    top = jnp.where(row < 4, up, turn(low, -side * half))
    low = turn(up, -2 * side * half)
    inside = lane < half
    return jnp.concatenate([jnp.where(inside, top, 0.0), jnp.where(inside, low, 0.0)], axis=0)


def correlate(w, bands, out, step=2, done=None):
    rows = w.shape[0]
    ch = out.shape[0]
    factor = 1.0 / math.sqrt(GROUP)
    both = jnp.concatenate([w[:, :BAND], w[:, MAXLAG:]], axis=0)
    width = step * MAXLAG
    for p in range(ch // step):
        r = jnp.dot(
            both, bands[:, p * width : (p + 1) * width], preferred_element_type=jnp.float32
        ) * factor
        for s in range(step):
            for h in range(2):
                out[step * p + s, :, h * MAXLAG : (h + 1) * MAXLAG] = r[
                    h * rows : (h + 1) * rows, s * MAXLAG : (s + 1) * MAXLAG
                ]
        if done is not None:
            done(p)


def gather_kernel(record_hbm, fir_hbm, result, rest, bands, record, fir, inner, outer, edges, near, leads, both,
                  window_up, down_one, down_two, one_edge, two_edges,
                  pair_one, pair_two, even_two, odd_two,
                  send, recv, ready):
    n, tn = lax.axis_size("chan"), lax.axis_size("tm")
    me, tm = lax.axis_index("chan"), lax.axis_index("tm")
    ch, length = record.shape
    tiles = length // TILE
    half = (fir.shape[1] - 1) // 2
    first, last = tm == 0, tm == tn - 1
    there = (jnp.logical_not(first), jnp.logical_not(last))
    step = (-1, 1, 0, 0)
    mirror = (1, 0, 2, 3)

    get_record = pltpu.make_async_copy(record_hbm, record, send.at[0])
    get_fir = pltpu.make_async_copy(fir_hbm, fir, send.at[1])
    get_record.start()
    get_fir.start()

    def each(d, act):
        if d < 2:
            pl.when(there[d])(act)
        else:
            act()

    def loop(low, high, act, sides=(0, 1, 2, 3)):
        def body(c, carry):
            for d in sides:
                act(c, d)
            return carry
        lax.fori_loop(low, high, body, 0)

    barrier = pltpu.get_barrier_semaphore()

    def signal(sem, c, d):
        each(d, lambda: pl.semaphore_signal(
            sem, inc=1, device_id=(c, tm + step[d]), device_id_type=MESH))

    signal(barrier, me, 1)
    loop(me + 1, n, lambda c, d: signal(barrier, c, d), (0, 1, 2))

    sides = 1 + jnp.minimum(tm, 1) + jnp.minimum(tn - 1 - tm, 1)
    earlier = jnp.minimum(tm, 1) + me * sides

    @pl.when(earlier > 0)
    def _():
        pl.semaphore_wait(barrier, earlier)

    signal(ready.at[me], me, 0)
    loop(0, me, lambda c, d: signal(ready.at[me], c, d), (2,))

    @pl.when(first)
    def _():
        near[0] = jnp.zeros(near.shape[1:], near.dtype)

    @pl.when(last)
    def _():
        near[1] = jnp.zeros(near.shape[1:], near.dtype)

    get_record.wait()
    get_fir.wait()
    pad = ROWS - ch
    taps = jnp.concatenate([fir[...], jnp.zeros((pad, fir.shape[1]), jnp.float32)], axis=0)
    x = jnp.concatenate([record[...].astype(jnp.float32), jnp.zeros((pad, length), jnp.float32)], axis=0)
    x = jnp.concatenate([x, jnp.zeros((ROWS, TILE), jnp.float32)], axis=1)
    y = whiten(x, taps, half)

    edge = y[:, length:]
    lane = lax.broadcasted_iota(jnp.int32, edge.shape, 1)
    lost = ((lane < half) & last) | ((lane >= TILE - half) & first)
    edge = jnp.where(lost, 0.0, edge)
    parts = [y[:, k * TILE : (k + 1) * TILE] for k in range(tiles)]
    edges[me, 0] = pack(parts[0], edge, half, -1).astype(jnp.bfloat16)
    edges[me, 1] = pack(parts[-1], edge, half, 1).astype(jnp.bfloat16)
    inner[me] = jnp.concatenate([part[:ch] for part in parts[1:-1]], axis=0).astype(jnp.bfloat16)

    def copy(c, d, slot, complete=False):
        if d < 2:
            source, target = edges.at[me, d], near.at[mirror[d], slot]
        else:
            ref = inner if d == 2 else outer if complete else edges
            source, target = ref.at[me], ref.at[slot]
        return pltpu.make_async_remote_copy(
            source, target, send.at[c // 2], recv.at[slot],
            device_id=(c, tm + step[d]), device_id_type=MESH,
        )

    def start(c, d):
        each(d, lambda: copy(c, d, me).start())

    def took(sem, ref):
        pltpu.make_async_copy(ref, ref, sem).wait()

    def took_sides(sem, one, two):
        pl.when(first | last)(lambda: took(sem, one))
        pl.when(there[0] & there[1])(lambda: took(sem, two))

    start(me, 0)
    loop(0, me, start)

    @pl.when(there[1])
    def _():
        pl.semaphore_wait(ready.at[me], 1)

    start(me, 1)

    def climb(low, high, call, parts):
        def body(c, carry):
            if call:
                pl.semaphore_wait(ready.at[c], 1)
            for d in parts:
                copy(c, d, me, True).start()
            return carry
        lax.fori_loop(low, high, body, 0)

    nearer = jnp.minimum(2 * (me // 2) + NEARER, n)
    climb(me + 1, nearer, True, (2,))

    def tile(ref, k):
        return ref[k].astype(jnp.float32)

    def sums(c):
        left, right = tile(near.at[0], c), tile(near.at[1], c)
        low, high = tile(edges.at[c], 0), tile(edges.at[c], 1)
        return [
            (left + unpack(low, half, -1))[:ch],
            (low + unpack(left, half, 1))[:ch],
            (high + unpack(right, half, -1))[:ch],
            (right + unpack(high, half, 1))[:ch],
        ]

    def joined(c):
        outer[c] = jnp.concatenate(sums(c), axis=0).astype(jnp.bfloat16)

    took_sides(recv.at[me], one_edge, two_edges)
    joined(me)
    climb(me + 1, nearer, False, (3,))
    later = jnp.where(me < 2, jnp.maximum(nearer, n - 2), n)
    climb(nearer, later, True, (2, 3))

    def window(c0, count):
        middle = [inner[c0 + q].astype(jnp.float32) for q in range(count)]
        ends = [outer[c0 + q].astype(jnp.float32) for q in range(count)]

        def rows(blocks, k):
            return jnp.concatenate([block[k * ch : (k + 1) * ch] for block in blocks], axis=0)

        lines = [rows(ends, k) for k in (0, 1)] + [rows(middle, k) for k in range(tiles - 2)]
        return lines + [rows(ends, k) for k in (2, 3)]

    flip = lax.broadcasted_iota(jnp.int32, (TILE, TILE), 0) + lax.broadcasted_iota(jnp.int32, (TILE, TILE), 1)
    flip = jnp.where(flip == TILE - 1, 1.0, 0.0).astype(jnp.bfloat16)
    lead = jnp.concatenate(
        [jnp.concatenate([part, jnp.zeros((pad, TILE), jnp.float32)], axis=0) for part in window(me, 1)[1:-1]], axis=0
    ).astype(jnp.bfloat16)
    lead = jnp.dot(lead, flip, preferred_element_type=jnp.float32)
    below = lax.broadcasted_iota(jnp.int32, (TILE, TILE), 0) >= lax.broadcasted_iota(jnp.int32, (TILE, TILE), 1)
    leads[...] = lead

    def spread_channel(i):
        column = pl.ds(pl.multiple_of(i * MAXLAG, MAXLAG), MAXLAG)
        before = jnp.zeros((TILE, TILE), jnp.float32)
        for k in range(tiles + 1):
            if k < tiles:
                row = leads[pl.ds(k * ROWS + i, 1), :]
                now = pltpu.roll(jnp.broadcast_to(row, (TILE, TILE)), 1, 1, stride=1, stride_axis=0)
            else:
                now = jnp.zeros((TILE, TILE), jnp.float32)
            bands[k * TILE : (k + 1) * TILE, column] = jnp.where(below, now, before).astype(jnp.bfloat16)
            before = now

    def spread_channels(step, carry):
        for i in range(TOGETHER):
            spread_channel(TOGETHER * step + i)
        return carry

    lax.fori_loop(0, ch // TOGETHER, spread_channels, 0)

    climb(later, n, True, (2, 3))

    def settle(c, carry):
        @pl.when(c < me)
        def _():
            took(recv.at[c], window_up)

        @pl.when(c > me)
        def _():
            took_sides(recv.at[c], down_one, down_two)
            joined(c)

        return carry

    middle = n // 2
    own_half = middle * (me // middle)
    lax.fori_loop(own_half, own_half + middle, settle, 0)
    rows = middle * ch
    w = jnp.concatenate(window(own_half, middle), axis=1).astype(jnp.bfloat16)
    both[...] = jnp.concatenate([w[:, :BAND], w[:, MAXLAG:]], axis=0)

    width = STEP * MAXLAG

    def correlate_some(p, carry):
        columns = pl.ds(pl.multiple_of(p * width, width), width)
        r = jnp.dot(both[...], bands[:, columns], preferred_element_type=jnp.float32)
        r = r * (1.0 / math.sqrt(GROUP))
        for s in range(STEP):
            for h in range(2):
                result[STEP * p + s, :, h * MAXLAG : (h + 1) * MAXLAG] = r[
                    h * rows : (h + 1) * rows, s * MAXLAG : (s + 1) * MAXLAG
                ]
        return carry

    lax.fori_loop(0, ch // STEP, correlate_some, 0)

    def sent_down(p, carry):
        took_sides(send.at[p], pair_one, pair_two)
        return carry

    def sent_up(p, carry):
        took(send.at[p], pair_one)
        return carry

    mine = me // 2
    lax.fori_loop(0, mine, sent_down, 0)
    pl.when(me % 2 == 0)(lambda: took_sides(send.at[mine], down_two, even_two))
    pl.when(me % 2 == 1)(lambda: took_sides(send.at[mine], down_two, odd_two))
    lax.fori_loop(mine + 1, n // 2, sent_up, 0)

    other = middle - own_half
    lax.fori_loop(other, other + middle, settle, 0)
    rest[...] = jnp.concatenate(window(other, middle), axis=1).astype(jnp.bfloat16)


def finish_kernel(early, rest, bands, out, late, sem):
    ch, rows = early.shape[:2]
    half = lax.axis_index("chan") // (lax.axis_size("chan") // 2)
    here = pl.ds(pl.multiple_of(half * rows, 8), rows)
    there = pl.ds(pl.multiple_of((1 - half) * rows, 8), rows)
    pltpu.make_async_copy(early, out.at[0, :, here], sem).start()

    def send(p):
        pair = slice(STEP * p, STEP * p + STEP)
        pltpu.make_async_copy(late.at[pair], out.at[0, pair, there], sem).start()

    correlate(rest[...], bands, late, STEP, send)
    pltpu.make_async_copy(out, out, sem).wait()


def local(record, fir):
    ch, length = record.shape
    n = lax.axis_size("chan")
    vmem = pl.BlockSpec(memory_space=pltpu.VMEM)
    hbm = pl.BlockSpec(memory_space=pltpu.HBM)
    tiles = length // TILE
    rows = n // 2 * ch
    held = pl.pallas_call(
        gather_kernel,
        out_shape=(
            pltpu.VMEM((ch, rows, LAGS), jnp.float32),
            pltpu.VMEM((rows, SPAN), jnp.bfloat16),
            pltpu.VMEM((BAND, ch * MAXLAG), jnp.bfloat16),
        ),
        in_specs=[hbm, hbm],
        out_specs=(vmem, vmem, vmem),
        scratch_shapes=[
            pltpu.VMEM((ch, length), jnp.bfloat16),
            pltpu.VMEM(fir.shape, jnp.float32),
            pltpu.VMEM((n, (tiles - 2) * ch, TILE), jnp.bfloat16),
            pltpu.VMEM((n, 4 * ch, TILE), jnp.bfloat16),
            pltpu.VMEM((n, 2, ROWS, TILE), jnp.bfloat16),
            pltpu.VMEM((2, n, ROWS, TILE), jnp.bfloat16),
            pltpu.VMEM((tiles * ROWS, TILE), jnp.float32),
            pltpu.VMEM((2 * rows, BAND), jnp.bfloat16),
            pltpu.VMEM(((tiles + 2) * ch, TILE), jnp.bfloat16),
            pltpu.VMEM(((tiles - 2) * ch + 3 * ROWS, TILE), jnp.bfloat16),
            pltpu.VMEM(((tiles - 2) * ch + 4 * ROWS, TILE), jnp.bfloat16),
            pltpu.VMEM((ROWS, TILE), jnp.bfloat16),
            pltpu.VMEM((2 * ROWS, TILE), jnp.bfloat16),
            pltpu.VMEM((2, (tiles + 2) * ch, TILE), jnp.bfloat16),
            pltpu.VMEM((2, (tiles - 2) * ch + 4 * ROWS, TILE), jnp.bfloat16),
            pltpu.VMEM(((tiles + 2) * ch + 2 * ROWS, TILE), jnp.bfloat16),
            pltpu.VMEM(((tiles - 2) * ch + 6 * ROWS, TILE), jnp.bfloat16),
            pltpu.SemaphoreType.DMA((n // 2,)),
            pltpu.SemaphoreType.DMA((n,)),
            pltpu.SemaphoreType.REGULAR((n,)),
        ],
        compiler_params=pltpu.CompilerParams(
            collective_id=0, has_side_effects=True, vmem_limit_bytes=24 << 20
        ),
    )(*(pltpu.with_memory_space_constraint(x, pltpu.HBM) for x in (record, fir)))
    return pl.pallas_call(
        finish_kernel,
        out_shape=jax.ShapeDtypeStruct((1, ch, n * ch, LAGS), jnp.float32),
        in_specs=[vmem, vmem, vmem],
        out_specs=pl.BlockSpec(memory_space=pl.ANY),
        scratch_shapes=[
            pltpu.VMEM((ch, rows, LAGS), jnp.float32),
            pltpu.SemaphoreType.DMA,
        ],
        compiler_params=pltpu.CompilerParams(vmem_limit_bytes=24 << 20),
    )(*held)


def solution(mesh):
    in_specs = (P("chan", "tm"), P("chan", None))
    out_specs = P("tm", "chan", None, None)
    return jax.shard_map(local, mesh=mesh, in_specs=in_specs, out_specs=out_specs, check_vma=False)
```

```python
import math

import jax
import jax.numpy as jnp
from jax import lax
from jax.experimental import pallas as pl
from jax.experimental.pallas import tpu as pltpu
from jax.sharding import PartitionSpec as P

GROUP = 512
MAXLAG = 128
LAGS = 2 * MAXLAG
SPAN = GROUP + LAGS
BAND = GROUP + MAXLAG
TILE = 128
ROWS = 16
NEARER = 4
STEP = 4
TOGETHER = 4
MESH = pl.DeviceIdType.MESH


def spread(taps):
    rows, count = taps.shape
    taps = jnp.concatenate([taps, jnp.zeros((rows, TILE - count), jnp.float32)], axis=1)
    high = taps.astype(jnp.bfloat16).astype(jnp.float32)
    lane = lax.broadcasted_iota(jnp.int32, taps.shape, 1)
    both = [
        jnp.concatenate([jnp.where(lane == k, part, 0.0) for part in (high, taps - high)], axis=1)
        for k in range(count)
    ]
    both = jnp.concatenate(both, axis=0).astype(jnp.bfloat16)
    ones = jnp.ones((2 * TILE, TILE), jnp.bfloat16)
    out = jnp.dot(both, ones, preferred_element_type=jnp.float32)
    return [out[k * rows : (k + 1) * rows] for k in range(count)]


def whiten(x, taps, half):
    width, count, steps = x.shape[1], taps.shape[1], 8
    taps = [jnp.concatenate([tap] * (width // TILE), axis=1) for tap in spread(taps)]
    moved = [pltpu.roll(x, (half - b) % width, 1) for b in range(steps)]
    total = None
    for a in range(0, count, steps):
        part = None
        for b in range(min(steps, count - a)):
            term = taps[a + b] * moved[b]
            part = term if part is None else part + term
        if a:
            part = pltpu.roll(part, width - a, 1)
        total = part if total is None else total + part
    return total


def turn(x, lanes):
    return pltpu.roll(x, lanes % TILE, 1)


def pack(tile, edge, half, side):
    row = lax.broadcasted_iota(jnp.int32, (8, TILE), 0)
    lane = lax.broadcasted_iota(jnp.int32, (8, TILE), 1)
    lane = TILE - 1 - lane if side < 0 else lane
    top, low = edge[:8], edge[8:]
    first = pltpu.roll(top, 4, 0)
    second = turn(top, side * half)
    third = turn(pltpu.roll(low, 4, 0), 2 * side * half)
    packed = jnp.where(lane < half, first, jnp.where(lane < 2 * half, second, third))
    return jnp.concatenate([tile[:8], jnp.where(row < 4, tile[8:], packed)], axis=0)


def unpack(tile, half, side):
    row = lax.broadcasted_iota(jnp.int32, (8, TILE), 0)
    lane = lax.broadcasted_iota(jnp.int32, (8, TILE), 1)
    lane = TILE - 1 - lane if side < 0 else lane
    low = tile[8:]
    up = pltpu.roll(low, 4, 0)
    top = jnp.where(row < 4, up, turn(low, -side * half))
    low = turn(up, -2 * side * half)
    inside = lane < half
    return jnp.concatenate([jnp.where(inside, top, 0.0), jnp.where(inside, low, 0.0)], axis=0)


def correlate(w, bands, out, step=2, done=None):
    rows = w.shape[0]
    ch = out.shape[0]
    factor = 1.0 / math.sqrt(GROUP)
    both = jnp.concatenate([w[:, :BAND], w[:, MAXLAG:]], axis=0)
    width = step * MAXLAG
    for p in range(ch // step):
        r = jnp.dot(
            both, bands[:, p * width : (p + 1) * width], preferred_element_type=jnp.float32
        ) * factor
        for s in range(step):
            for h in range(2):
                out[step * p + s, :, h * MAXLAG : (h + 1) * MAXLAG] = r[
                    h * rows : (h + 1) * rows, s * MAXLAG : (s + 1) * MAXLAG
                ]
        if done is not None:
            done(p)


def gather_kernel(record_hbm, fir_hbm, result, rest, bands, record, fir, inner, outer, edges, near, leads, both,
                  window_up, down_one, down_two, one_edge, two_edges,
                  pair_one, pair_two, even_two, odd_two,
                  send, recv, ready):
    n, tn = lax.axis_size("chan"), lax.axis_size("tm")
    me, tm = lax.axis_index("chan"), lax.axis_index("tm")
    ch, length = record.shape
    tiles = length // TILE
    half = (fir.shape[1] - 1) // 2
    first, last = tm == 0, tm == tn - 1
    there = (jnp.logical_not(first), jnp.logical_not(last))
    step = (-1, 1, 0, 0)
    mirror = (1, 0, 2, 3)

    get_record = pltpu.make_async_copy(record_hbm, record, send.at[0])
    get_fir = pltpu.make_async_copy(fir_hbm, fir, send.at[1])
    get_record.start()
    get_fir.start()

    def each(d, act):
        if d < 2:
            pl.when(there[d])(act)
        else:
            act()

    def loop(low, high, act, sides=(0, 1, 2, 3)):
        def body(c, carry):
            for d in sides:
                act(c, d)
            return carry
        lax.fori_loop(low, high, body, 0)

    barrier = pltpu.get_barrier_semaphore()

    def signal(sem, c, d):
        each(d, lambda: pl.semaphore_signal(
            sem, inc=1, device_id=(c, tm + step[d]), device_id_type=MESH))

    signal(barrier, me, 1)
    loop(me + 1, n, lambda c, d: signal(barrier, c, d), (0, 1, 2))

    sides = 1 + jnp.minimum(tm, 1) + jnp.minimum(tn - 1 - tm, 1)
    earlier = jnp.minimum(tm, 1) + me * sides

    @pl.when(earlier > 0)
    def _():
        pl.semaphore_wait(barrier, earlier)

    signal(ready.at[me], me, 0)
    loop(0, me, lambda c, d: signal(ready.at[me], c, d), (2,))

    @pl.when(first)
    def _():
        near[0] = jnp.zeros(near.shape[1:], near.dtype)

    @pl.when(last)
    def _():
        near[1] = jnp.zeros(near.shape[1:], near.dtype)

    get_record.wait()
    get_fir.wait()
    pad = ROWS - ch
    taps = jnp.concatenate([fir[...], jnp.zeros((pad, fir.shape[1]), jnp.float32)], axis=0)
    x = jnp.concatenate([record[...].astype(jnp.float32), jnp.zeros((pad, length), jnp.float32)], axis=0)
    x = jnp.concatenate([x, jnp.zeros((ROWS, TILE), jnp.float32)], axis=1)
    y = whiten(x, taps, half)

    edge = y[:, length:]
    lane = lax.broadcasted_iota(jnp.int32, edge.shape, 1)
    lost = ((lane < half) & last) | ((lane >= TILE - half) & first)
    edge = jnp.where(lost, 0.0, edge)
    parts = [y[:, k * TILE : (k + 1) * TILE] for k in range(tiles)]
    edges[me, 0] = pack(parts[0], edge, half, -1).astype(jnp.bfloat16)
    edges[me, 1] = pack(parts[-1], edge, half, 1).astype(jnp.bfloat16)
    inner[me] = jnp.concatenate([part[:ch] for part in parts[1:-1]], axis=0).astype(jnp.bfloat16)

    def copy(c, d, slot, complete=False):
        if d < 2:
            source, target = edges.at[me, d], near.at[mirror[d], slot]
        else:
            ref = inner if d == 2 else outer if complete else edges
            source, target = ref.at[me], ref.at[slot]
        return pltpu.make_async_remote_copy(
            source, target, send.at[c // 2], recv.at[slot],
            device_id=(c, tm + step[d]), device_id_type=MESH,
        )

    def start(c, d):
        each(d, lambda: copy(c, d, me).start())

    def took(sem, ref):
        pltpu.make_async_copy(ref, ref, sem).wait()

    def took_sides(sem, one, two):
        pl.when(first | last)(lambda: took(sem, one))
        pl.when(there[0] & there[1])(lambda: took(sem, two))

    start(me, 0)
    loop(0, me, start)

    @pl.when(there[1])
    def _():
        pl.semaphore_wait(ready.at[me], 1)

    start(me, 1)

    def climb(low, high, call, parts):
        def body(c, carry):
            if call:
                pl.semaphore_wait(ready.at[c], 1)
            for d in parts:
                copy(c, d, me, True).start()
            return carry
        lax.fori_loop(low, high, body, 0)

    nearer = jnp.minimum(2 * (me // 2) + NEARER, n)
    climb(me + 1, nearer, True, (2,))

    def tile(ref, k):
        return ref[k].astype(jnp.float32)

    def sums(c):
        left, right = tile(near.at[0], c), tile(near.at[1], c)
        low, high = tile(edges.at[c], 0), tile(edges.at[c], 1)
        return [
            (left + unpack(low, half, -1))[:ch],
            (low + unpack(left, half, 1))[:ch],
            (high + unpack(right, half, -1))[:ch],
            (right + unpack(high, half, 1))[:ch],
        ]

    def joined(c):
        outer[c] = jnp.concatenate(sums(c), axis=0).astype(jnp.bfloat16)

    took_sides(recv.at[me], one_edge, two_edges)
    joined(me)
    climb(me + 1, nearer, False, (3,))
    later = jnp.where(me < 2, jnp.maximum(nearer, n - 2), n)
    climb(nearer, later, True, (2, 3))

    def window(c0, count):
        middle = [inner[c0 + q].astype(jnp.float32) for q in range(count)]
        ends = [outer[c0 + q].astype(jnp.float32) for q in range(count)]

        def rows(blocks, k):
            return jnp.concatenate([block[k * ch : (k + 1) * ch] for block in blocks], axis=0)

        lines = [rows(ends, k) for k in (0, 1)] + [rows(middle, k) for k in range(tiles - 2)]
        return lines + [rows(ends, k) for k in (2, 3)]

    flip = lax.broadcasted_iota(jnp.int32, (TILE, TILE), 0) + lax.broadcasted_iota(jnp.int32, (TILE, TILE), 1)
    flip = jnp.where(flip == TILE - 1, 1.0, 0.0).astype(jnp.bfloat16)
    lead = jnp.concatenate(
        [jnp.concatenate([part, jnp.zeros((pad, TILE), jnp.float32)], axis=0) for part in window(me, 1)[1:-1]], axis=0
    ).astype(jnp.bfloat16)
    lead = jnp.dot(lead, flip, preferred_element_type=jnp.float32)
    below = lax.broadcasted_iota(jnp.int32, (TILE, TILE), 0) >= lax.broadcasted_iota(jnp.int32, (TILE, TILE), 1)
    leads[...] = lead

    def spread_channel(i):
        column = pl.ds(pl.multiple_of(i * MAXLAG, MAXLAG), MAXLAG)
        before = jnp.zeros((TILE, TILE), jnp.float32)
        for k in range(tiles + 1):
            if k < tiles:
                row = leads[pl.ds(k * ROWS + i, 1), :]
                now = pltpu.roll(jnp.broadcast_to(row, (TILE, TILE)), 1, 1, stride=1, stride_axis=0)
            else:
                now = jnp.zeros((TILE, TILE), jnp.float32)
            bands[k * TILE : (k + 1) * TILE, column] = jnp.where(below, now, before).astype(jnp.bfloat16)
            before = now

    def spread_channels(step, carry):
        for i in range(TOGETHER):
            spread_channel(TOGETHER * step + i)
        return carry

    lax.fori_loop(0, ch // TOGETHER, spread_channels, 0)

    climb(later, n, True, (2, 3))

    def settle(c, carry):
        @pl.when(c < me)
        def _():
            took(recv.at[c], window_up)

        @pl.when(c > me)
        def _():
            took_sides(recv.at[c], down_one, down_two)
            joined(c)

        return carry

    middle = n // 2
    own_half = middle * (me // middle)
    lax.fori_loop(own_half, own_half + middle, settle, 0)
    rows = middle * ch
    w = jnp.concatenate(window(own_half, middle), axis=1).astype(jnp.bfloat16)
    both[...] = jnp.concatenate([w[:, :BAND], w[:, MAXLAG:]], axis=0)

    width = STEP * MAXLAG

    def correlate_some(p, carry):
        columns = pl.ds(pl.multiple_of(p * width, width), width)
        r = jnp.dot(both[...], bands[:, columns], preferred_element_type=jnp.float32)
        r = r * (1.0 / math.sqrt(GROUP))
        for s in range(STEP):
            for h in range(2):
                result[STEP * p + s, :, h * MAXLAG : (h + 1) * MAXLAG] = r[
                    h * rows : (h + 1) * rows, s * MAXLAG : (s + 1) * MAXLAG
                ]
        return carry

    lax.fori_loop(0, ch // STEP, correlate_some, 0)

    def sent_down(p, carry):
        took_sides(send.at[p], pair_one, pair_two)
        return carry

    def sent_up(p, carry):
        took(send.at[p], pair_one)
        return carry

    other = middle - own_half
    lax.fori_loop(other, other + middle, settle, 0)
    rest[...] = jnp.concatenate(window(other, middle), axis=1).astype(jnp.bfloat16)

    mine = me // 2
    lax.fori_loop(0, mine, sent_down, 0)
    pl.when(me % 2 == 0)(lambda: took_sides(send.at[mine], down_two, even_two))
    pl.when(me % 2 == 1)(lambda: took_sides(send.at[mine], down_two, odd_two))
    lax.fori_loop(mine + 1, n // 2, sent_up, 0)


def finish_kernel(early, rest, bands, out, late, sem):
    ch, rows = early.shape[:2]
    half = lax.axis_index("chan") // (lax.axis_size("chan") // 2)
    here = pl.ds(pl.multiple_of(half * rows, 8), rows)
    there = pl.ds(pl.multiple_of((1 - half) * rows, 8), rows)
    pltpu.make_async_copy(early, out.at[0, :, here], sem).start()

    def send(p):
        pair = slice(STEP * p, STEP * p + STEP)
        pltpu.make_async_copy(late.at[pair], out.at[0, pair, there], sem).start()

    correlate(rest[...], bands, late, STEP, send)
    pltpu.make_async_copy(out, out, sem).wait()


def local(record, fir):
    ch, length = record.shape
    n = lax.axis_size("chan")
    vmem = pl.BlockSpec(memory_space=pltpu.VMEM)
    hbm = pl.BlockSpec(memory_space=pltpu.HBM)
    tiles = length // TILE
    rows = n // 2 * ch
    held = pl.pallas_call(
        gather_kernel,
        out_shape=(
            pltpu.VMEM((ch, rows, LAGS), jnp.float32),
            pltpu.VMEM((rows, SPAN), jnp.bfloat16),
            pltpu.VMEM((BAND, ch * MAXLAG), jnp.bfloat16),
        ),
        in_specs=[hbm, hbm],
        out_specs=(vmem, vmem, vmem),
        scratch_shapes=[
            pltpu.VMEM((ch, length), jnp.bfloat16),
            pltpu.VMEM(fir.shape, jnp.float32),
            pltpu.VMEM((n, (tiles - 2) * ch, TILE), jnp.bfloat16),
            pltpu.VMEM((n, 4 * ch, TILE), jnp.bfloat16),
            pltpu.VMEM((n, 2, ROWS, TILE), jnp.bfloat16),
            pltpu.VMEM((2, n, ROWS, TILE), jnp.bfloat16),
            pltpu.VMEM((tiles * ROWS, TILE), jnp.float32),
            pltpu.VMEM((2 * rows, BAND), jnp.bfloat16),
            pltpu.VMEM(((tiles + 2) * ch, TILE), jnp.bfloat16),
            pltpu.VMEM(((tiles - 2) * ch + 3 * ROWS, TILE), jnp.bfloat16),
            pltpu.VMEM(((tiles - 2) * ch + 4 * ROWS, TILE), jnp.bfloat16),
            pltpu.VMEM((ROWS, TILE), jnp.bfloat16),
            pltpu.VMEM((2 * ROWS, TILE), jnp.bfloat16),
            pltpu.VMEM((2, (tiles + 2) * ch, TILE), jnp.bfloat16),
            pltpu.VMEM((2, (tiles - 2) * ch + 4 * ROWS, TILE), jnp.bfloat16),
            pltpu.VMEM(((tiles + 2) * ch + 2 * ROWS, TILE), jnp.bfloat16),
            pltpu.VMEM(((tiles - 2) * ch + 6 * ROWS, TILE), jnp.bfloat16),
            pltpu.SemaphoreType.DMA((n // 2,)),
            pltpu.SemaphoreType.DMA((n,)),
            pltpu.SemaphoreType.REGULAR((n,)),
        ],
        compiler_params=pltpu.CompilerParams(
            collective_id=0, has_side_effects=True, vmem_limit_bytes=24 << 20
        ),
    )(*(pltpu.with_memory_space_constraint(x, pltpu.HBM) for x in (record, fir)))
    return pl.pallas_call(
        finish_kernel,
        out_shape=jax.ShapeDtypeStruct((1, ch, n * ch, LAGS), jnp.float32),
        in_specs=[vmem, vmem, vmem],
        out_specs=pl.BlockSpec(memory_space=pl.ANY),
        scratch_shapes=[
            pltpu.VMEM((ch, rows, LAGS), jnp.float32),
            pltpu.SemaphoreType.DMA,
        ],
        compiler_params=pltpu.CompilerParams(vmem_limit_bytes=24 << 20),
    )(*held)


def solution(mesh):
    in_specs = (P("chan", "tm"), P("chan", None))
    out_specs = P("tm", "chan", None, None)
    return jax.shard_map(local, mesh=mesh, in_specs=in_specs, out_specs=out_specs, check_vma=False)
```
